128 devices in a mesh: expert: 8 (over x, core), shard: 16 (over z, y).
Axes of the slice: x: 4, y: 4, z: 4, core: 2. Of those that a mesh axis runs over, the one named last changes fastest.
Arguments:
- tokens_in: bfloat16 [4096, 4096], P(('expert', 'shard')), may hold values from -6 to 6
- out_grad: bfloat16 [4096, 2, 8192], P(('expert', 'shard')), may hold values from -6 to 6
- expert_ids: int32 [4096, 2], P(('expert', 'shard')), may hold values from 0 to 7, all different within a row; in each aligned block of 32 rows (0 to 31, 32 to 63, ...) at most 10 rows name the same one
- d_levels: int32 [8, 16], P('expert'), may hold values from 0 to 7
- f_levels: int32 [8, 32], P('expert', 'shard'), may hold values from 0 to 7
Outputs:
- ascent: bfloat16 [8, 4096, 8192], P('expert', None, 'shard')
The draws below stay inside these ranges and needn't reach their ends.
Inputs may be any that keep to these rules, and one draw needn't show every extreme that they name: `expert_ids`: each token names two different experts; among the 64 entries of one device no expert is named more than 10 times, and 10 is reached on some device; every expert is named somewhere.
All inputs are finite; a program needn't handle non-finite values.
Results may differ from the reference program's by a relative error of at most 0.001.
Values may be sent and summed in bfloat16 or wider, within the bound.
No kernel may reach another device: no remote copies, remote signals or barrier semaphores. Data moves between devices by JAX's collectives and lax.ppermute only.
A program may use at most 128 MiB of HBM per device.

```python
import math
import jax
import jax.numpy as jnp
import numpy as np
from jax import lax

D = 4096
FF = 8192
BLK = 256
TOK_DEV = 32
EXPERTS = 8
CAP = 10
TOKENS = 4096
N_EXPERT = 8
N_SHARD = 16


def place_ends(values, own_key, least, high):
    longest = values.shape.index(max(values.shape))
    spots = []
    for shift in (0, 1):
        where = [jax.random.randint(jax.random.fold_in(own_key, axis), (), 0, length) for axis, length in enumerate(values.shape)]
        where[longest] = (where[longest] + shift) % values.shape[longest]
        spots.append(tuple(where))
    return values.at[spots[0]].set(least).at[spots[1]].set(high)


def block_scale(rng, dims, cuts, low, high):
    def one(dim, parts):
        steps = jax.random.uniform(jax.random.fold_in(jax.random.fold_in(rng, 6), dim), (parts,), jnp.float32, low / len(cuts), high / len(cuts))
        return jnp.repeat(jnp.exp(steps), dims[dim] // parts).reshape((-1,) + (1,) * (len(dims) - dim - 1))

    loudness = one(*cuts[0])
    for cut in cuts[1:]:
        loudness = loudness * one(*cut)
    return loudness


def assign_block(rng, own, number, rows, count, top, reach, lean):
    sequence = jax.random.permutation(rng, count)
    packed, usual = portions_of(count, rows * top, reach, lean, True), portions_of(count, rows * top, reach, lean, False)
    places = jnp.arange(count)

    def named(tallies, turn):
        used = int((tallies > 0).sum())
        fixed = max(1, used // 4)
        moved = fixed + (places - fixed + turn * (used - fixed)) % max(1, count - fixed)
        return jnp.zeros((count,), jnp.int32).at[sequence[jnp.where(places < fixed, places, moved)]].set(jnp.asarray(tallies, jnp.int32))

    tallies = jnp.where(number % 4 == 0, named(packed, number // 4), named(usual, number - number // 4 - 1))
    mixed = jax.random.permutation(jax.random.fold_in(own, 3), count)
    giver, sink = mixed[0:count // 2 * 2:2], mixed[1:count // 2 * 2:2]
    room = jnp.minimum(tallies[giver] - 1, reach - tallies[sink]) // 2
    room = jnp.where((giver == sequence[0]) | (sink == sequence[0]) | (tallies[sink] == 0), 0, jnp.maximum(room, 0))
    moved = jax.random.randint(jax.random.fold_in(own, 4), (count // 2,), 0, 1 << 20) % (room + 1)
    tallies = tallies.at[giver].add(-moved).at[sink].add(moved)
    members = jnp.searchsorted(jnp.cumsum(tallies), jnp.arange(rows * top), side="right").astype(jnp.int32)
    grid = members.reshape(top, rows).T
    grid = grid[jax.random.permutation(jax.random.fold_in(own, 1), rows)]
    turn = jax.random.randint(jax.random.fold_in(own, 2), (rows, 1), 0, top)
    return jnp.take_along_axis(grid, (jnp.arange(top)[None, :] + turn) % top, axis=1)


def portions_of(count, total, bound, slope, full):
    loads = [(1 << 20) // math.isqrt(rank ** slope) + 1 for rank in range(1, count + 1)]
    largest = bound if full else min(bound, max(-(-total // count), total * loads[0] // sum(loads)))
    least = 1 if total - largest >= count - 1 else 0
    counts, spare = [largest] + [least] * (count - 1), total - largest - least * (count - 1)
    while spare > 0:
        movable = [i for i in range(1, count) if counts[i] < largest] or [i for i in range(1, count) if counts[i] < bound]
        whole, remaining = sum([loads[i] for i in movable]), spare
        for i in movable:
            addition = min(bound - counts[i], max(1, remaining * loads[i] // whole), spare)
            counts[i] = counts[i] + addition
            spare = spare - addition
    return np.array(counts)


def normal_values(own_key, shape, scale, bound, shards=(), held_as=jnp.bfloat16):
    values = scale * jax.random.normal(own_key, shape, jnp.float32)
    if shards:
        values = values * block_scale(own_key, shape, shards, -0.22, 0.18)
    return jnp.clip(values, -bound, bound).astype(held_as)


def setup_inputs(seed: int = 0) -> dict:
    splits = jax.random.split(jax.random.key(seed), 6)
    tokens_in = normal_values(splits[0], (TOKENS, D), 1.0, 6.0, ((0, 128),))
    out_grad = normal_values(splits[1], (TOKENS, 2, FF), 1.0, 6.0, ((0, 128),))
    expert_ids_keys = jax.random.split(jax.random.fold_in(splits[2], 1), TOKENS // TOK_DEV)
    expert_ids_turns = jax.random.permutation(jax.random.fold_in(splits[2], 3), TOKENS // TOK_DEV)
    expert_ids = jax.vmap(lambda own, number: assign_block(jax.random.fold_in(splits[2], 2), own, number, TOK_DEV, EXPERTS, 2, CAP, 2))(expert_ids_keys, expert_ids_turns).reshape((TOKENS, 2))
    d_levels = place_ends(jax.random.randint(splits[3], (EXPERTS, D // BLK), 0, 8), jax.random.fold_in(splits[3], 1), 0, 7).astype(jnp.int32)
    f_levels = place_ends(jax.random.randint(splits[4], (EXPERTS, FF // BLK), 0, 8), jax.random.fold_in(splits[4], 1), 0, 7).astype(jnp.int32)
    return {"tokens_in": tokens_in, "out_grad": out_grad, "expert_ids": expert_ids, "d_levels": d_levels, "f_levels": f_levels}


def invert_blocks(blocks):
    lower = jnp.linalg.cholesky(blocks)
    identity = jnp.eye(blocks.shape[-1], dtype=blocks.dtype)
    return jax.vmap(lambda factor: jax.scipy.linalg.cho_solve((factor, True), identity))(lower)

def damping(levels):
    return 0.05 * jnp.exp(0.4 * levels.astype(jnp.float32))

def reference(tokens_in, out_grad, expert_ids, d_levels, f_levels):
    row_limit = N_EXPERT * N_SHARD * CAP
    flat_ids = expert_ids.reshape(-1)
    tok_index = (jnp.arange(2 * TOKENS, dtype=jnp.int32) // 2).astype(jnp.int32)
    grads_flat = out_grad.reshape(2 * TOKENS, FF)
    highest = lax.Precision.HIGHEST

    def per_expert(inputs):
        expert, d_row, f_row = inputs
        chosen = flat_ids == expert
        ordering = jnp.argsort(jnp.where(chosen, 0, 1).astype(jnp.int32), stable=True)[:row_limit].astype(jnp.int32)
        live_rows = chosen[ordering].astype(jnp.bfloat16)
        row_count = jnp.sum(chosen.astype(jnp.float32))
        x_rows = tokens_in[tok_index[ordering]] * live_rows[:, None]
        g_rows = grads_flat[ordering] * live_rows[:, None]
        gradient = jnp.dot(x_rows.T.astype(jnp.float32), g_rows.astype(jnp.float32), preferred_element_type=jnp.float32)
        x_blocks = x_rows.astype(jnp.float32).reshape(row_limit, D // BLK, BLK)
        g_blocks = g_rows.astype(jnp.float32).reshape(row_limit, FF // BLK, BLK)
        identity = jnp.eye(BLK, dtype=jnp.float32)
        cov_a = jnp.einsum('rbi,rbj->bij', x_blocks, x_blocks, precision=highest) / row_count
        cov_a = cov_a + damping(d_row)[:, None, None] * identity
        cov_f = jnp.einsum('rbi,rbj->bij', g_blocks, g_blocks, precision=highest) / row_count
        cov_f = cov_f + damping(f_row)[:, None, None] * identity
        inv_a = invert_blocks(cov_a)
        inv_f = invert_blocks(cov_f)
        left_done = jnp.einsum('bij,bjf->bif', inv_a, gradient.reshape(D // BLK, BLK, FF), precision=highest)
        precond = jnp.einsum('dcj,cjk->dck', left_done.reshape(D, FF // BLK, BLK), inv_f, precision=highest)
        return precond.reshape(D, FF)
    precond = lax.map(per_expert, (jnp.arange(EXPERTS, dtype=jnp.int32), d_levels, f_levels))
    norm_total = jnp.sum(precond * precond)
    ascent_scale = lax.rsqrt(norm_total / (EXPERTS * D * FF) + 1e-06)
    return (precond * ascent_scale).astype(jnp.bfloat16)
```

```python
import functools

import jax
import jax.numpy as jnp
from jax import lax
from jax.experimental import pallas as pl
from jax.experimental.pallas import tpu as pltpu
from jax.sharding import PartitionSpec as P

BLK = 256
BASE = 32
PANEL = 8
F32 = jnp.float32
BF = jnp.bfloat16
TN = (((0,), (0,)), ((), ()))
VMEM = 56 << 20
PARAMS = pltpu.CompilerParams(vmem_limit_bytes=VMEM)


def iota(shape, dim):
    return lax.broadcasted_iota(jnp.int32, shape, dim)


def div(value, by):
    return (value * (65536 // by + 1)) >> 16


def onehot(hit):
    return jnp.where(hit, 1.0, 0.0).astype(BF)


def split2(x):
    high = x.astype(BF)
    return high, (x - high.astype(F32)).astype(BF)


def split3(x):
    high = x.astype(BF)
    rest = x - high.astype(F32)
    mid = rest.astype(BF)
    return high, mid, (rest - mid.astype(F32)).astype(BF)


def tn_full(a, b):
    ah, am, al = split3(a)
    bh, bm, bl = split3(b)
    return lax.dot_general(
        jnp.concatenate([ah, ah, am, ah, al, am], 0),
        jnp.concatenate([bh, bm, bh, bl, bh, bm], 0),
        TN,
        preferred_element_type=F32,
    )


def dot3(a, b):
    ah, al = a
    bh, bl = b
    dot = functools.partial(jnp.dot, preferred_element_type=F32)
    return dot(ah, bh) + (dot(ah, bl) + dot(al, bh))


def invert_base(packs):
    lane, sub = iota((BASE, 128), 1), iota((BASE, 128), 0)
    start = (lane // BASE) * BASE
    inner = lane - start
    packs = list(packs)
    for k0 in range(0, BASE, PANEL):
        cols = [
            [jnp.take_along_axis(x, start + (k0 + j), axis=1) for j in range(PANEL)] for x in packs
        ]
        for j in range(PANEL):
            k = k0 + j
            is_col, is_row = inner == k, sub == k
            for g, x in enumerate(packs):
                col = cols[g][j]
                inv = 1.0 / col[k : k + 1, :]
                row = jnp.where(is_col[:1], 1.0, x[k : k + 1, :]) * inv
                for jj in range(j + 1, PANEL):
                    other = cols[g][jj]
                    scaled = other[k : k + 1, :] * inv
                    cols[g][jj] = jnp.where(is_row, scaled, other - col * scaled)
                packs[g] = jnp.where(is_row, row, jnp.where(is_col, 0.0, x) - col * row)
    return packs


def invert_all(m_ref, count):
    per = 128 // BASE
    lane, sub = iota((BASE, BLK), 1), iota((BASE, BLK), 0)
    wide = iota((BLK, BLK), 1)
    for low in range(0, BLK, BASE):
        end = low + BASE
        packs = [
            jnp.concatenate(
                [m_ref[min(g + j, count - 1), low:end, low:end] for j in range(per)], axis=1
            )
            for g in range(0, count, per)
        ]
        packs = invert_base(packs)
        own = (lane >= low) & (lane < end)
        minus_eye = jnp.where(lane - low == sub, -1.0, 0.0)
        for m in range(count):
            at = (m % per) * BASE
            pivot = packs[m // per][:, at : at + BASE]
            rows = m_ref[m, low:end, :]
            new_rows = tn_full(pivot, jnp.where(own, minus_eye, rows))
            change = tn_full(jnp.where(own, 0.0, rows), new_rows)
            m_ref[m] = jnp.where((wide >= low) & (wide < end), 0.0, m_ref[m]) - change
            m_ref[m, low:end, :] = new_rows


def slots(id_col, id_row, first, step, capacity):
    shape = (id_col.shape[0], id_row.shape[1])
    earlier = iota(shape, 0) < first + step * iota(shape, 1)
    same = (id_col == id_row) & earlier
    rank = jnp.sum(jnp.where(same, 1, 0), axis=0, keepdims=True)
    return id_row, rank


def send_x_kernel(cap, parts, col_ref, first_ref, second_ref, x_ref, out_ref):
    rows, toks = out_ref.shape[0], x_ref.shape[0]
    width = x_ref.shape[1] // parts
    per = cap * parts
    hot = []
    for part in range(parts):
        total = None
        for j, ids in enumerate((first_ref, second_ref)):
            expert, rank = slots(col_ref[...], ids[...], j, 2, cap)
            target = expert * per + part * cap + rank
            hit = jnp.where(iota((rows, toks), 0) == target, 1.0, 0.0)
            total = hit if total is None else total + hit
        hot.append(total.astype(BF))
    data = jnp.concatenate([x_ref[:, p * width : (p + 1) * width] for p in range(parts)], 0)
    out_ref[...] = jnp.dot(
        jnp.concatenate(hot, 1), data, preferred_element_type=F32
    ).astype(BF)


def take_x_kernel(cap, parts, in_ref, out_ref):
    groups, per, width = in_ref.shape
    data = in_ref[...].reshape(groups * per, width)
    shape = (groups * cap, groups * per)
    row = iota(shape, 0)
    source = div(row, cap)
    base = source * per + (row - source * cap)
    for part in range(parts):
        pick = onehot(iota(shape, 1) == base + part * cap)
        out_ref[:, part * width : (part + 1) * width] = jnp.dot(
            pick, data, preferred_element_type=F32
        ).astype(BF)


def payload_kernel(cap, rows, nx, ng, col_ref, row_ref, first_ref, second_ref, x_ref, g_ref,
                   out_ref, hot_ref, add_ref):
    groups = out_ref.shape[1]
    toks, pairs = x_ref.shape[0], g_ref.shape[0]
    total = groups * rows

    @pl.when(pl.program_id(0) == 0)
    def _():
        for part in range(nx):
            hit = None
            for j, ids in enumerate((first_ref, second_ref)):
                expert, rank = slots(col_ref[...], ids[...], j, 2, cap)
                target = expert * rows + part * cap + rank
                one = jnp.where(iota((total, toks), 0) == target, 1.0, 0.0)
                hit = one if hit is None else hit + one
            hot_ref[:, part * toks : (part + 1) * toks] = hit.astype(BF)
        expert, rank = slots(col_ref[...], row_ref[...], 0, 1, cap)
        for part in range(ng):
            target = expert * rows + (nx + part) * cap + rank
            low = nx * toks + part * pairs
            hot_ref[:, low : low + pairs] = onehot(iota((total, pairs), 0) == target)
        row = iota((total, pairs), 0)
        mine = (row >> (rows.bit_length() - 1)) == row_ref[...]
        marked = (row & (rows - 1)) == (nx + ng) * cap
        add_ref[...] = jnp.sum(jnp.where(mine & marked, 1.0, 0.0), axis=1, keepdims=True)

    data = jnp.concatenate(
        [x_ref[:, p * 128 : (p + 1) * 128] for p in range(nx)]
        + [g_ref[:, p * 128 : (p + 1) * 128] for p in range(ng)],
        0,
    )
    out = jnp.dot(hot_ref[...], data, preferred_element_type=F32) + add_ref[...]
    out_ref[...] = out.astype(BF).reshape(groups, rows, 128)[None]


def inverse_kernel(cap, nx, ng, lev_ref, in_ref, a_ref, s_ref, h_ref, x_ref, m_ref):
    shards, groups, rows, _ = in_ref.shape
    live = groups * cap
    shape = (live, groups * rows)
    row = iota(shape, 0)
    source = div(row, cap)
    base = source * rows + (row - source * cap)
    pick = jnp.concatenate(
        [onehot(iota(shape, 1) == base + part * cap) for part in range(nx + ng)], 0
    )
    total = jnp.zeros((1, 128), F32)
    mark = (nx + ng) * cap
    for s in range(shards):
        data = in_ref[s].reshape(groups * rows, 128)
        got = jnp.dot(pick, data, preferred_element_type=F32).astype(BF)
        for part in range(nx + ng):
            piece = got[part * live : (part + 1) * live]
            if part < nx:
                x_ref[s * live : (s + 1) * live, part * 128 : (part + 1) * 128] = piece
            else:
                h_ref[s, :, (part - nx) * 128 : (part - nx + 1) * 128] = piece
        for g in range(groups):
            total = total + in_ref[s, g, mark : mark + 1, :].astype(F32)
    scale = 1.0 / total[:, :1]
    eye = iota((BLK, BLK), 0) == iota((BLK, BLK), 1)
    width = h_ref.shape[2]
    h = h_ref[...].reshape(shards * live, width)
    for m in range(1 + width // BLK):
        part = x_ref[...] if m == 0 else h[:, (m - 1) * BLK : m * BLK]
        cov = lax.dot_general(part, part, TN, preferred_element_type=F32)
        damp = 0.05 * jnp.exp(0.4 * jnp.full((1, 1), lev_ref[m], F32))
        m_ref[m] = cov * scale + jnp.where(eye, damp, 0.0)
    invert_all(m_ref, m_ref.shape[0])
    a_ref[...] = -m_ref[0]
    s_ref[...] = -m_ref[1:]


def product_kernel(block_ref, x_ref, h_ref, a_ref, s_ref, out_ref, sum_ref):
    step = pl.program_id(0)
    shards, live, width = h_ref.shape
    h = h_ref[...].reshape(shards * live, width)
    x = x_ref[...].reshape(shards * live, BLK)
    gradient = lax.dot_general(x, h, TN, preferred_element_type=F32)
    left = split2(a_ref[0])
    total = jnp.zeros((8, 128), F32)
    for c in range(width // BLK):
        cut = slice(c * BLK, (c + 1) * BLK)
        right = dot3(split2(gradient[:, cut]), split2(s_ref[c]))
        out = dot3(left, split2(right))
        out_ref[:, cut] = out
        square = (out * out).reshape(BLK // 8, 8, BLK).sum(axis=0)
        for k in range(BLK // 128):
            total = total + square[:, k * 128 : (k + 1) * 128]

    @pl.when(step == 0)
    def _():
        sum_ref[...] = jnp.zeros_like(sum_ref)

    sum_ref[...] += total


def scale_kernel(count, norm_ref, in_ref, out_ref):
    total = jnp.sum(jnp.sum(norm_ref[...], axis=0, keepdims=True), axis=1, keepdims=True)
    out_ref[...] = (in_ref[...] * lax.rsqrt(total / count + 1e-06)).astype(BF)


def shift(n, rest, by, inner):
    pairs = []
    for hi in range(n):
        for lo in range(rest):
            src = hi * rest + lo
            if inner:
                pairs.append((src, hi * rest + (lo + by) % rest))
            else:
                pairs.append((src, ((hi + by) % n) * rest + lo))
    return pairs


def full(shape):
    return pl.BlockSpec(shape, lambda *_: (0,) * len(shape))


def local(tokens_in, out_grad, expert_ids, d_levels, f_levels):
    groups, shards = lax.axis_size("expert"), lax.axis_size("shard")
    toks, width = tokens_in.shape
    ff = out_grad.shape[2]
    ff_dev = ff // shards
    cap = min(toks, max(2, 5 * toks // (2 * groups)))
    live = groups * cap
    own = width // shards
    parts = 4
    nx, ng = own // 128, ff_dev // 128
    rows = 64
    call = functools.partial(pl.pallas_call, compiler_params=PARAMS)

    id_row = expert_ids.reshape(1, 2 * toks)
    id_col = expert_ids.reshape(2 * toks, 1)
    first, second = expert_ids[:, 0].reshape(1, toks), expert_ids[:, 1].reshape(1, toks)

    x_send = call(
        functools.partial(send_x_kernel, cap, parts),
        out_shape=jax.ShapeDtypeStruct((groups * cap * parts, width // parts), BF),
        name="send_x",
    )(id_col, first, second, tokens_in)
    x_recv = lax.all_to_all(
        x_send.reshape(groups, cap * parts, width // parts), "expert", 0, 0, tiled=True
    )
    x_group = call(
        functools.partial(take_x_kernel, cap, parts),
        out_shape=jax.ShapeDtypeStruct((live, width), BF),
        name="take_x",
    )(x_recv)
    rows_x = lax.all_gather(x_group[None], "shard", axis=0, tiled=True)

    payload = call(
        functools.partial(payload_kernel, cap, rows, nx, ng),
        out_shape=jax.ShapeDtypeStruct((shards, groups, rows, 128), BF),
        grid=(shards,),
        in_specs=[
            full((2 * toks, 1)),
            full((1, 2 * toks)),
            full((1, toks)),
            full((1, toks)),
            pl.BlockSpec((toks, own), lambda s: (0, s)),
            pl.BlockSpec((2 * toks, ff_dev), lambda s: (0, s)),
        ],
        out_specs=pl.BlockSpec((1, groups, rows, 128), lambda s: (s, 0, 0, 0)),
        scratch_shapes=[
            pltpu.VMEM((groups * rows, nx * toks + ng * 2 * toks), BF),
            pltpu.VMEM((groups * rows, 1), F32),
        ],
        name="payload",
    )(id_col, id_row, first, second, tokens_in, out_grad.reshape(2 * toks, ff))
    received = lax.all_to_all(
        payload.reshape(shards * groups, rows, 128), ("shard", "expert"), 0, 0, tiled=True
    ).reshape(shards, groups, rows, 128)

    me = lax.axis_index("shard")
    levels = jnp.concatenate(
        [lax.dynamic_slice_in_dim(d_levels[0], me, 1, 0), f_levels[0]]
    ).astype(F32)
    vm = pl.BlockSpec(memory_space=pltpu.VMEM)
    inv_a, inv_f, rows_g = call(
        functools.partial(inverse_kernel, cap, nx, ng),
        out_shape=(
            jax.ShapeDtypeStruct((BLK, BLK), F32),
            jax.ShapeDtypeStruct((ff_dev // BLK, BLK, BLK), F32),
            jax.ShapeDtypeStruct((shards, live, ff_dev), BF),
        ),
        in_specs=[pl.BlockSpec(memory_space=pltpu.SMEM), vm],
        out_specs=(vm, vm, vm),
        scratch_shapes=[
            pltpu.VMEM((shards * live, own), BF),
            pltpu.VMEM((1 + ff_dev // BLK, BLK, BLK), F32),
        ],
        name="inverse",
    )(levels, received)

    side = 4
    outer = shards // side
    send = functools.partial(lax.ppermute, axis_name="shard")
    line = jnp.stack(
        [inv_a] + [send(inv_a, perm=shift(outer, side, k, True)) for k in range(1, side)]
    )
    plane = jnp.concatenate(
        [line] + [send(line, perm=shift(outer, side, k, False)) for k in range(1, outer)], 0
    )
    order = jnp.arange(shards, dtype=jnp.int32)
    up, across = order // side, order % side
    block_of = ((me // side - up) % outer) * side + (me % side - across) % side

    precond, square = call(
        product_kernel,
        out_shape=(
            jax.ShapeDtypeStruct((width, ff_dev), F32),
            jax.ShapeDtypeStruct((8, 128), F32),
        ),
        grid_spec=pltpu.PrefetchScalarGridSpec(
            num_scalar_prefetch=1,
            grid=(shards,),
            in_specs=[
                pl.BlockSpec((shards, live, BLK), lambda i, b: (0, 0, b[i])),
                full((shards, live, ff_dev)),
                pl.BlockSpec((1, BLK, BLK), lambda i, b: (i, 0, 0)),
                full((ff_dev // BLK, BLK, BLK)),
            ],
            out_specs=(
                pl.BlockSpec((BLK, ff_dev), lambda i, b: (b[i], 0)),
                full((8, 128)),
            ),
        ),
        name="product",
    )(block_of, rows_x, rows_g, plane, inv_f)

    norm = jnp.sum(square, axis=0, keepdims=True)
    norm = lax.all_to_all(jnp.broadcast_to(norm, (groups, 128)), "expert", 0, 0, tiled=True)
    norm = jnp.sum(norm, axis=0, keepdims=True)
    norm = lax.all_to_all(jnp.broadcast_to(norm, (shards, 128)), "shard", 0, 0, tiled=True)
    tile = width // 8
    ascent = call(
        functools.partial(scale_kernel, float(groups * width * ff)),
        out_shape=jax.ShapeDtypeStruct((width, ff_dev), BF),
        grid=(8,),
        in_specs=[full((shards, 128)), pl.BlockSpec((tile, ff_dev), lambda i: (i, 0))],
        out_specs=pl.BlockSpec((tile, ff_dev), lambda i: (i, 0)),
        name="scale",
    )(norm, precond)
    return ascent[None]


def solution(mesh):
    return jax.shard_map(
        local,
        mesh=mesh,
        in_specs=(
            P(("expert", "shard"), None),
            P(("expert", "shard"), None, None),
            P(("expert", "shard"), None),
            P("expert", None),
            P("expert", "shard"),
        ),
        out_specs=P("expert", None, "shard"),
        check_vma=False,
    )
```

```python
import functools

import jax
import jax.numpy as jnp
from jax import lax
from jax.experimental import pallas as pl
from jax.experimental.pallas import tpu as pltpu
from jax.sharding import PartitionSpec as P

BLK = 256
BASE = 32
PANEL = 8
F32 = jnp.float32
BF = jnp.bfloat16
TN = (((0,), (0,)), ((), ()))


def iota(shape, dim):
    return lax.broadcasted_iota(jnp.int32, shape, dim)


def div(value, by):
    return (value * (65536 // by + 1)) >> 16


def onehot(hit):
    return jnp.where(hit, 1.0, 0.0).astype(BF)


def split2(x):
    high = x.astype(BF)
    return high, (x - high.astype(F32)).astype(BF)


def split3(x):
    high = x.astype(BF)
    rest = x - high.astype(F32)
    mid = rest.astype(BF)
    return high, mid, (rest - mid.astype(F32)).astype(BF)


def tn_full(a, b):
    ah, am, al = split3(a)
    bh, bm, bl = split3(b)
    return lax.dot_general(
        jnp.concatenate([ah, ah, am, ah, al, am], 0),
        jnp.concatenate([bh, bm, bh, bl, bh, bm], 0),
        TN,
        preferred_element_type=F32,
    )


def dot3(a, b):
    ah, al = a
    bh, bl = b
    dot = functools.partial(jnp.dot, preferred_element_type=F32)
    return dot(ah, bh) + (dot(ah, bl) + dot(al, bh))


def invert_base(packs):
    lane, sub = iota((BASE, 128), 1), iota((BASE, 128), 0)
    start = (lane // BASE) * BASE
    inner = lane - start
    packs = list(packs)
    for k0 in range(0, BASE, PANEL):
        cols = [
            [jnp.take_along_axis(x, start + (k0 + j), axis=1) for j in range(PANEL)] for x in packs
        ]
        for j in range(PANEL):
            k = k0 + j
            is_col, is_row = inner == k, sub == k
            for g, x in enumerate(packs):
                col = cols[g][j]
                inv = 1.0 / col[k : k + 1, :]
                row = jnp.where(is_col[:1], 1.0, x[k : k + 1, :]) * inv
                for jj in range(j + 1, PANEL):
                    other = cols[g][jj]
                    scaled = other[k : k + 1, :] * inv
                    cols[g][jj] = jnp.where(is_row, scaled, other - col * scaled)
                packs[g] = jnp.where(is_row, row, jnp.where(is_col, 0.0, x) - col * row)
    return packs


def invert_all(m_ref, count):
    per = 128 // BASE
    lane, sub = iota((BASE, BLK), 1), iota((BASE, BLK), 0)
    wide = iota((BLK, BLK), 1)
    for low in range(0, BLK, BASE):
        end = low + BASE
        packs = [
            jnp.concatenate(
                [m_ref[min(g + j, count - 1), low:end, low:end] for j in range(per)], axis=1
            )
            for g in range(0, count, per)
        ]
        packs = invert_base(packs)
        own = (lane >= low) & (lane < end)
        minus_eye = jnp.where(lane - low == sub, -1.0, 0.0)
        for m in range(count):
            at = (m % per) * BASE
            pivot = packs[m // per][:, at : at + BASE]
            rows = m_ref[m, low:end, :]
            new_rows = tn_full(pivot, jnp.where(own, minus_eye, rows))
            change = tn_full(jnp.where(own, 0.0, rows), new_rows)
            m_ref[m] = jnp.where((wide >= low) & (wide < end), 0.0, m_ref[m]) - change
            m_ref[m, low:end, :] = new_rows


def slots(id_col, id_row, first, step, capacity):
    shape = (id_col.shape[0], id_row.shape[1])
    earlier = iota(shape, 0) < first + step * iota(shape, 1)
    same = (id_col == id_row) & earlier
    rank = jnp.sum(jnp.where(same, 1, 0), axis=0, keepdims=True)
    return id_row, rank


def send_x_kernel(cap, parts, col_ref, first_ref, second_ref, x_ref, out_ref):
    rows, toks = out_ref.shape[0], x_ref.shape[0]
    width = x_ref.shape[1] // parts
    per = cap * parts
    hot = []
    for part in range(parts):
        total = None
        for j, ids in enumerate((first_ref, second_ref)):
            expert, rank = slots(col_ref[...], ids[...], j, 2, cap)
            target = expert * per + part * cap + rank
            hit = jnp.where(iota((rows, toks), 0) == target, 1.0, 0.0)
            total = hit if total is None else total + hit
        hot.append(total.astype(BF))
    data = jnp.concatenate([x_ref[:, p * width : (p + 1) * width] for p in range(parts)], 0)
    out_ref[...] = jnp.dot(
        jnp.concatenate(hot, 1), data, preferred_element_type=F32
    ).astype(BF)


def take_x_kernel(cap, parts, in_ref, *out_refs):
    groups, per, width = in_ref.shape
    data = in_ref[...].reshape(groups * per, width)
    shape = (groups * cap, groups * per)
    row = iota(shape, 0)
    source = div(row, cap)
    base = source * per + (row - source * cap)
    for part in range(parts):
        pick = onehot(iota(shape, 1) == base + part * cap)
        half, at = divmod(part, parts // len(out_refs))
        out_refs[half][:, at * width : (at + 1) * width] = jnp.dot(
            pick, data, preferred_element_type=F32
        ).astype(BF)


def payload_kernel(cap, rows, nx, ng, col_ref, row_ref, first_ref, second_ref, x_ref, g_ref,
                   out_ref, hot_ref, add_ref):
    groups = out_ref.shape[1]
    toks, pairs = x_ref.shape[0], g_ref.shape[0]
    total = groups * rows

    @pl.when(pl.program_id(0) == 0)
    def _():
        for part in range(nx):
            hit = None
            for j, ids in enumerate((first_ref, second_ref)):
                expert, rank = slots(col_ref[...], ids[...], j, 2, cap)
                target = expert * rows + part * cap + rank
                one = jnp.where(iota((total, toks), 0) == target, 1.0, 0.0)
                hit = one if hit is None else hit + one
            hot_ref[:, part * toks : (part + 1) * toks] = hit.astype(BF)
        expert, rank = slots(col_ref[...], row_ref[...], 0, 1, cap)
        for part in range(ng):
            target = expert * rows + (nx + part) * cap + rank
            low = nx * toks + part * pairs
            hot_ref[:, low : low + pairs] = onehot(iota((total, pairs), 0) == target)
        row = iota((total, pairs), 0)
        mine = (row >> (rows.bit_length() - 1)) == row_ref[...]
        marked = (row & (rows - 1)) == (nx + ng) * cap
        add_ref[...] = jnp.sum(jnp.where(mine & marked, 1.0, 0.0), axis=1, keepdims=True)

    pair = out_ref.shape[0]

    def lanes(ref, part, each):
        cuts = [(t * each + part) * 128 for t in range(pair)]
        return jnp.concatenate([ref[:, at : at + 128] for at in cuts], 1)

    data = jnp.concatenate(
        [lanes(x_ref, p, nx) for p in range(nx)] + [lanes(g_ref, p, ng) for p in range(ng)], 0
    )
    out = jnp.dot(hot_ref[...], data, preferred_element_type=F32) + add_ref[...]
    for t in range(pair):
        piece = out[:, t * 128 : (t + 1) * 128].astype(BF)
        out_ref[t] = piece.reshape(groups, rows, 128)


def inverse_kernel(cap, nx, ng, rel_ref, lev_ref, in_ref, q_ref, p_ref, s_ref, one_ref, two_ref,
                   x_ref, m_ref):
    groups, shards, rows, _ = in_ref.shape
    live = groups * cap
    shape = (live, groups * rows)
    row = iota(shape, 0)
    source = div(row, cap)
    base = source * rows + (row - source * cap)
    pick = jnp.concatenate(
        [onehot(iota(shape, 1) == base + part * cap) for part in range(nx + ng)], 0
    )
    total = jnp.zeros((1, 128), F32)
    mark = (nx + ng) * cap
    for s in range(shards):
        data = in_ref[:, s].reshape(groups * rows, 128)
        got = jnp.dot(pick, data, preferred_element_type=F32).astype(BF)
        for part in range(nx):
            x_ref[s * live : (s + 1) * live, part * 128 : (part + 1) * 128] = got[
                part * live : (part + 1) * live
            ]
        h = jnp.concatenate(
            [got[part * live : (part + 1) * live] for part in range(nx, nx + ng)], 1
        )
        one_ref[rel_ref[s]] = h
        two_ref[rel_ref[shards + s]] = h
        for g in range(groups):
            total = total + in_ref[g, s, mark : mark + 1, :].astype(F32)
    scale = 1.0 / total[:, :1]
    eye = iota((BLK, BLK), 0) == iota((BLK, BLK), 1)
    width = one_ref.shape[2]
    h = one_ref[...].reshape(shards * live, width)
    for m in range(1 + width // BLK):
        part = x_ref[...] if m == 0 else h[:, (m - 1) * BLK : m * BLK]
        cov = lax.dot_general(part, part, TN, preferred_element_type=F32)
        damp = 0.05 * jnp.exp(0.4 * jnp.full((1, 1), lev_ref[m], F32))
        m_ref[m] = cov * scale + jnp.where(eye, damp, 0.0)
    invert_all(m_ref, m_ref.shape[0])
    s_ref[...] = -m_ref[1:]
    half = BLK // 2
    top, low = -m_ref[0, :half, :half], -m_ref[0, half:, half:]
    down, across = iota((half, half), 0), iota((half, half), 1)
    q_ref[:half] = -m_ref[0, :half, half:]
    diag = jnp.sum(jnp.where(down == across, low, 0.0), axis=0, keepdims=True)
    q_ref[half:] = jnp.broadcast_to(diag, (8, half))
    p_ref[...] = jnp.where(down >= across, top, low)


def unfold(q_ref, p_ref):
    half = p_ref.shape[1]
    quarter, diag, both = q_ref[0, :half], q_ref[0, half : half + 1], p_ref[0]
    down, across = iota((half, half), 0), iota((half, half), 1)
    lower = jnp.where(down > across, both, 0.0)
    upper = jnp.where(down < across, both, 0.0)
    eye = down == across
    top = lower + lower.T + jnp.where(eye, both, 0.0)
    low = upper + upper.T + jnp.where(eye, diag, 0.0)
    return jnp.concatenate(
        [jnp.concatenate([top, quarter], 1), jnp.concatenate([quarter.T, low], 1)], 0
    )


def product_kernel(pieces, rel_ref, *refs):
    x_refs, refs = (refs[:pieces], refs[pieces : 2 * pieces]), refs[2 * pieces :]
    h_refs, q_refs, p_refs = refs[0:2], refs[2:4], refs[4:6]
    s_ref, out_refs, sum_ref = refs[6], refs[7:9], refs[9]
    width = h_refs[0].shape[2]
    total = jnp.zeros((8, 128), F32)
    for half in range(2):
        x = jnp.concatenate([ref[...] for ref in x_refs[half]], 0)
        h = h_refs[half][...].reshape(x.shape[0], width)
        gradient = lax.dot_general(x, h, TN, preferred_element_type=F32)
        left = split2(unfold(q_refs[half], p_refs[half]))
        for c in range(width // BLK):
            cut = slice(c * BLK, (c + 1) * BLK)
            right = dot3(split2(gradient[:, cut]), split2(s_ref[c]))
            out = dot3(left, split2(right))
            out_refs[half][:, cut] = out
            square = (out * out).reshape(BLK // 8, 8, BLK).sum(axis=0)
            for k in range(BLK // 128):
                total = total + square[:, k * 128 : (k + 1) * 128]

    @pl.when(pl.program_id(0) == 0)
    def _():
        sum_ref[...] = jnp.zeros_like(sum_ref)

    sum_ref[...] += total


def scale_kernel(count, norm_ref, one_ref, two_ref, out_ref):
    total = jnp.sum(jnp.sum(norm_ref[...], axis=0, keepdims=True), axis=1, keepdims=True)
    scale = lax.rsqrt(total / count + 1e-06)
    out_ref[0] = (one_ref[...] * scale).astype(BF)
    out_ref[1] = (two_ref[...] * scale).astype(BF)


SIDE = 4


def send(array, by, inner):
    pairs = []
    for at in range(SIDE * SIDE):
        out, inn = at // SIDE, at % SIDE
        if inner:
            pairs.append((at, out * SIDE + (inn + by) % SIDE))
        else:
            pairs.append((at, (out + by) % SIDE * SIDE + inn))
    return lax.ppermute(array, "shard", pairs)


def gather(array, inner):
    line = jnp.concatenate([array] + [send(array, k, inner) for k in range(1, SIDE)], 0)
    half = line.shape[0] // 2
    before, after = send(line, 1, not inner), send(line, SIDE - 1, not inner)
    far = [send(before[:half], 1, not inner), send(after[half:], SIDE - 1, not inner)]
    return [line, before, *far, after]


def full(shape):
    return pl.BlockSpec(shape, lambda *_: (0,) * len(shape))


def local(tokens_in, out_grad, expert_ids, d_levels, f_levels):
    groups, shards = lax.axis_size("expert"), lax.axis_size("shard")
    toks, width = tokens_in.shape
    ff = out_grad.shape[2]
    ff_dev = ff // shards
    cap = min(toks, max(2, 5 * toks // (2 * groups)))
    live = groups * cap
    own = width // shards
    parts = 4
    nx, ng = own // 128, ff_dev // 128
    rows = 64

    def call(kernel, mib=16, **kwargs):
        params = pltpu.CompilerParams(vmem_limit_bytes=mib << 20)
        return pl.pallas_call(kernel, compiler_params=params, **kwargs)

    id_row = expert_ids.reshape(1, 2 * toks)
    id_col = expert_ids.reshape(2 * toks, 1)
    first, second = expert_ids[:, 0].reshape(1, toks), expert_ids[:, 1].reshape(1, toks)

    x_send = call(
        functools.partial(send_x_kernel, cap, parts),
        out_shape=jax.ShapeDtypeStruct((groups * cap * parts, width // parts), BF),
        name="send_x",
    )(id_col, first, second, tokens_in)
    x_recv = lax.all_to_all(
        x_send.reshape(groups, cap * parts, width // parts), "expert", 0, 0, tiled=True
    )
    x_one, x_two = call(
        functools.partial(take_x_kernel, cap, parts),
        out_shape=[jax.ShapeDtypeStruct((live, width // 2), BF)] * 2,
        name="take_x",
    )(x_recv)
    x_one, x_two = gather(x_one, True), gather(x_two, False)

    payload = call(
        functools.partial(payload_kernel, cap, rows, nx, ng),
        out_shape=jax.ShapeDtypeStruct((shards, groups, rows, 128), BF),
        grid=(shards // 2,),
        in_specs=[
            full((2 * toks, 1)),
            full((1, 2 * toks)),
            full((1, toks)),
            full((1, toks)),
            pl.BlockSpec((toks, 2 * own), lambda s: (0, s)),
            pl.BlockSpec((2 * toks, 2 * ff_dev), lambda s: (0, s)),
        ],
        out_specs=pl.BlockSpec((2, groups, rows, 128), lambda s: (s, 0, 0, 0)),
        scratch_shapes=[
            pltpu.VMEM((groups * rows, nx * toks + ng * 2 * toks), BF),
            pltpu.VMEM((groups * rows, 1), F32),
        ],
        name="payload",
    )(id_col, id_row, first, second, tokens_in, out_grad.reshape(2 * toks, ff))
    received = lax.all_to_all(payload, "shard", 0, 0, tiled=True).transpose(1, 0, 2, 3)
    received = lax.all_to_all(received, "expert", 0, 0, tiled=True)

    me = lax.axis_index("shard")
    order = jnp.arange(shards, dtype=jnp.int32)
    back_out = (me // SIDE - order // SIDE) % SIDE
    back_in = (me % SIDE - order % SIDE) % SIDE
    place = jnp.concatenate([back_out * SIDE + back_in, back_in * SIDE + back_out])
    levels = jnp.concatenate(
        [lax.dynamic_slice_in_dim(d_levels[0], me, 1, 0), f_levels[0]]
    ).astype(F32)
    vm, sm = pl.BlockSpec(memory_space=pltpu.VMEM), pl.BlockSpec(memory_space=pltpu.SMEM)
    half = BLK // 2
    quarter, folded, inv_f, *rows_g = call(
        functools.partial(inverse_kernel, cap, nx, ng),
        mib=24,
        out_shape=(
            jax.ShapeDtypeStruct((half + 8, half), F32),
            jax.ShapeDtypeStruct((half, half), F32),
            jax.ShapeDtypeStruct((ff_dev // BLK, BLK, BLK), F32),
            jax.ShapeDtypeStruct((shards, live, ff_dev), BF),
            jax.ShapeDtypeStruct((shards, live, ff_dev), BF),
        ),
        in_specs=[sm, sm, vm],
        out_specs=(vm,) * 5,
        scratch_shapes=[
            pltpu.VMEM((shards * live, own), BF),
            pltpu.VMEM((1 + ff_dev // BLK, BLK, BLK), F32),
        ],
        name="inverse",
    )(place, levels, received)
    quarter = jnp.concatenate(gather(quarter, True), 0).reshape(shards, half + 8, half)
    folded = jnp.concatenate(gather(folded, False), 0).reshape(shards, half, half)

    steps = shards // 2

    def columns(pieces):
        return [pl.BlockSpec((p.shape[0], BLK), lambda i, r: (0, i)) for p in pieces]

    one, two, square = call(
        functools.partial(product_kernel, len(x_one)),
        mib=24,
        out_shape=(
            jax.ShapeDtypeStruct((width // 2, ff_dev), F32),
            jax.ShapeDtypeStruct((width // 2, ff_dev), F32),
            jax.ShapeDtypeStruct((8, 128), F32),
        ),
        grid_spec=pltpu.PrefetchScalarGridSpec(
            num_scalar_prefetch=1,
            grid=(steps,),
            in_specs=[
                *columns(x_one),
                *columns(x_two),
                full((shards, live, ff_dev)),
                full((shards, live, ff_dev)),
                pl.BlockSpec((1, half + 8, half), lambda i, r: (r[i], 0, 0)),
                pl.BlockSpec((1, half + 8, half), lambda i, r: (r[steps + i], 0, 0)),
                pl.BlockSpec((1, half, half), lambda i, r: (r[shards + i], 0, 0)),
                pl.BlockSpec((1, half, half), lambda i, r: (r[shards + steps + i], 0, 0)),
                full((ff_dev // BLK, BLK, BLK)),
            ],
            out_specs=(
                pl.BlockSpec((BLK, ff_dev), lambda i, r: (i, 0)),
                pl.BlockSpec((BLK, ff_dev), lambda i, r: (i, 0)),
                full((8, 128)),
            ),
        ),
        name="product",
    )(place, *x_one, *x_two, *rows_g, quarter, quarter, folded, folded, inv_f)

    norm = jnp.sum(square, axis=0, keepdims=True)
    norm = lax.all_to_all(jnp.broadcast_to(norm, (groups, 128)), "expert", 0, 0, tiled=True)
    norm = jnp.sum(norm, axis=0, keepdims=True)
    norm = lax.all_to_all(jnp.broadcast_to(norm, (shards, 128)), "shard", 0, 0, tiled=True)
    tile = width // 8
    ascent = call(
        functools.partial(scale_kernel, float(groups * width * ff)),
        out_shape=jax.ShapeDtypeStruct((2, width // 2, ff_dev), BF),
        grid=(4,),
        in_specs=[full((shards, 128))]
        + [pl.BlockSpec((tile, ff_dev), lambda i: (i, 0))] * 2,
        out_specs=pl.BlockSpec((2, tile, ff_dev), lambda i: (0, i, 0)),
        name="scale",
    )(norm, one, two)
    return ascent.reshape(1, width, ff_dev)


def solution(mesh):
    return jax.shard_map(
        local,
        mesh=mesh,
        in_specs=(
            P(("expert", "shard"), None),
            P(("expert", "shard"), None, None),
            P(("expert", "shard"), None),
            P("expert", None),
            P("expert", "shard"),
        ),
        out_specs=P("expert", None, "shard"),
        check_vma=False,
    )
```

```python
import functools

import jax
import jax.numpy as jnp
from jax import lax
from jax.experimental import pallas as pl
from jax.experimental.pallas import tpu as pltpu
from jax.sharding import PartitionSpec as P

BLK = 256
BASE = 32
PANEL = 8
F32 = jnp.float32
BF = jnp.bfloat16
TN = (((0,), (0,)), ((), ()))


def iota(shape, dim):
    return lax.broadcasted_iota(jnp.int32, shape, dim)


def div(value, by):
    return (value * (65536 // by + 1)) >> 16


def onehot(hit):
    return jnp.where(hit, 1.0, 0.0).astype(BF)


def split2(x):
    high = x.astype(BF)
    return high, (x - high.astype(F32)).astype(BF)


def split3(x):
    high = x.astype(BF)
    rest = x - high.astype(F32)
    mid = rest.astype(BF)
    return high, mid, (rest - mid.astype(F32)).astype(BF)


def tn_full(a, b):
    ah, am, al = split3(a)
    bh, bm, bl = split3(b)
    return lax.dot_general(
        jnp.concatenate([ah, ah, am, ah, al, am], 0),
        jnp.concatenate([bh, bm, bh, bl, bh, bm], 0),
        TN,
        preferred_element_type=F32,
    )


def dot3(a, b):
    ah, al = a
    bh, bl = b
    return jnp.dot(
        jnp.concatenate([ah, ah, al], 1),
        jnp.concatenate([bh, bl, bh], 0),
        preferred_element_type=F32,
    )


def invert_base(packs):
    lane, sub = iota((BASE, 128), 1), iota((BASE, 128), 0)
    start = (lane // BASE) * BASE
    inner = lane - start
    packs = list(packs)
    for k0 in range(0, BASE, PANEL):
        cols = [
            [jnp.take_along_axis(x, start + (k0 + j), axis=1) for j in range(PANEL)] for x in packs
        ]
        for j in range(PANEL):
            k = k0 + j
            is_col, is_row = inner == k, sub == k
            for g, x in enumerate(packs):
                col = cols[g][j]
                inv = 1.0 / col[k : k + 1, :]
                row = jnp.where(is_col[:1], 1.0, x[k : k + 1, :]) * inv
                for jj in range(j + 1, PANEL):
                    other = cols[g][jj]
                    scaled = other[k : k + 1, :] * inv
                    cols[g][jj] = jnp.where(is_row, scaled, other - col * scaled)
                packs[g] = jnp.where(is_row, row, jnp.where(is_col, 0.0, x) - col * row)
    return packs


def invert_all(m_ref, count):
    per = 128 // BASE
    lane, sub = iota((BASE, BLK), 1), iota((BASE, BLK), 0)
    wide = iota((BLK, BLK), 1)
    for low in range(0, BLK, BASE):
        end = low + BASE
        packs = [
            jnp.concatenate(
                [m_ref[min(g + j, count - 1), low:end, low:end] for j in range(per)], axis=1
            )
            for g in range(0, count, per)
        ]
        packs = invert_base(packs)
        own = (lane >= low) & (lane < end)
        minus_eye = jnp.where(lane - low == sub, -1.0, 0.0)
        for m in range(count):
            at = (m % per) * BASE
            pivot = packs[m // per][:, at : at + BASE]
            rows = m_ref[m, low:end, :]
            new_rows = tn_full(pivot, jnp.where(own, minus_eye, rows))
            change = tn_full(jnp.where(own, 0.0, rows), new_rows)
            m_ref[m] = jnp.where((wide >= low) & (wide < end), 0.0, m_ref[m]) - change
            m_ref[m, low:end, :] = new_rows


def slots(id_col, id_row, first, step, capacity):
    shape = (id_col.shape[0], id_row.shape[1])
    earlier = iota(shape, 0) < first + step * iota(shape, 1)
    same = (id_col == id_row) & earlier
    rank = jnp.sum(jnp.where(same, 1, 0), axis=0, keepdims=True)
    return id_row, rank


def send_x_kernel(cap, parts, col_ref, first_ref, second_ref, x_ref, out_ref):
    rows, toks = out_ref.shape[0], x_ref.shape[0]
    width = x_ref.shape[1] // parts
    per = cap * parts
    hot = []
    for part in range(parts):
        total = None
        for j, ids in enumerate((first_ref, second_ref)):
            expert, rank = slots(col_ref[...], ids[...], j, 2, cap)
            target = expert * per + part * cap + rank
            hit = jnp.where(iota((rows, toks), 0) == target, 1.0, 0.0)
            total = hit if total is None else total + hit
        hot.append(total.astype(BF))
    data = jnp.concatenate([x_ref[:, p * width : (p + 1) * width] for p in range(parts)], 0)
    out_ref[...] = jnp.dot(
        jnp.concatenate(hot, 1), data, preferred_element_type=F32
    ).astype(BF)


def take_x_kernel(cap, parts, in_ref, *out_refs):
    groups, per, width = in_ref.shape
    data = in_ref[...].reshape(groups * per, width)
    shape = (groups * cap, groups * per)
    row = iota(shape, 0)
    source = div(row, cap)
    base = source * per + (row - source * cap)
    for part in range(parts):
        pick = onehot(iota(shape, 1) == base + part * cap)
        rest = part * width
        got = jnp.dot(pick, data, preferred_element_type=F32).astype(BF)
        for ref in out_refs:
            if 0 <= rest < ref.shape[1]:
                ref[:, rest : rest + width] = got
            rest -= ref.shape[1]


def payload_kernel(cap, rows, ng, col_ref, row_ref, g_ref, out_ref, hot_ref, add_ref):
    pair, groups = out_ref.shape[:2]
    pairs = g_ref.shape[0]
    total = groups * rows

    @pl.when(pl.program_id(0) == 0)
    def _():
        expert, rank = slots(col_ref[...], row_ref[...], 0, 1, cap)
        row = iota((total, pairs), 0)
        for part in range(ng):
            target = expert * rows + part * cap + rank
            hot_ref[:, part * pairs : (part + 1) * pairs] = onehot(row == target)
        marked = row == row_ref[...] * rows + ng * cap
        add_ref[...] = jnp.sum(jnp.where(marked, 1.0, 0.0), axis=1, keepdims=True)

    data = jnp.concatenate(
        [
            jnp.concatenate(
                [g_ref[:, (t * ng + p) * 128 : (t * ng + p + 1) * 128] for t in range(pair)], 1
            )
            for p in range(ng)
        ],
        0,
    )
    out = jnp.dot(hot_ref[...], data, preferred_element_type=F32) + add_ref[...]
    for t in range(pair):
        piece = out[:, t * 128 : (t + 1) * 128].astype(BF)
        out_ref[t] = piece.reshape(groups, rows, 128)


def rows_kernel(cap, ng, rel_ref, in_ref, h_ref, one_ref, two_ref, count_ref):
    shards, groups, rows, _ = in_ref.shape
    live = groups * cap
    shape = (live, groups * rows)
    row = iota(shape, 0)
    source = div(row, cap)
    base = source * rows + (row - source * cap)
    pick = jnp.concatenate([onehot(iota(shape, 1) == base + p * cap) for p in range(ng)], 0)
    total = jnp.zeros((1, 128), F32)
    for s in range(shards):
        data = in_ref[s].reshape(groups * rows, 128)
        got = jnp.dot(pick, data, preferred_element_type=F32).astype(BF)
        h = jnp.concatenate([got[p * live : (p + 1) * live] for p in range(ng)], 1)
        h_ref[s] = h
        one_ref[rel_ref[s]] = h
        two_ref[rel_ref[shards + s]] = h
        for g in range(groups):
            total = total + in_ref[s, g, ng * cap : ng * cap + 1, :].astype(F32)
    count_ref[...] = total


def chunk_kernel(sizes, first, lev_ref, count_ref, *refs):
    x_refs = []
    for size in sizes:
        x_refs.append(refs[:size])
        refs = refs[size:]
    h_refs, refs = refs[: len(sizes)], refs[len(sizes) :]
    if first:
        out_ref, sum_ref, s_ref, m_ref = refs
    else:
        s_ref, out_ref, sum_ref, m_ref = refs
    width = out_ref.shape[1]
    cuts = [slice(c * BLK, (c + 1) * BLK) for c in range(width // BLK)]
    scale = 1.0 / count_ref[:, :1]
    eye = iota((BLK, BLK), 0) == iota((BLK, BLK), 1)

    def set_block(at, cov):
        damp = 0.05 * jnp.exp(0.4 * jnp.full((1, 1), lev_ref[at], F32))
        m_ref[at] = cov * scale + jnp.where(eye, damp, 0.0)

    block = 0
    for pieces, h_ref in zip(x_refs, h_refs):
        h = h_ref[...].reshape(-1, width)
        for at in range(0, pieces[0].shape[1], BLK):
            x = jnp.concatenate([ref[:, at : at + BLK] for ref in pieces], 0)
            both = lax.dot_general(
                x, jnp.concatenate([x, h], 1), TN, preferred_element_type=F32
            )
            set_block(block, both[:, :BLK])
            out_ref[block * BLK : (block + 1) * BLK, :] = both[:, BLK:]
            block += 1
    if first:
        h = h_refs[0][...].reshape(-1, width)
        for c, cut in enumerate(cuts):
            part = h[:, cut]
            set_block(block + c, lax.dot_general(part, part, TN, preferred_element_type=F32))
    invert_all(m_ref, m_ref.shape[0])
    if first:
        for c in range(len(cuts)):
            s_ref[c] = -m_ref[block + c]
    right = [split2(s_ref[c]) for c in range(len(cuts))]
    total = jnp.zeros((8, 128), F32)
    for b in range(block):
        rows = slice(b * BLK, (b + 1) * BLK)
        left = split2(-m_ref[b])
        for c, cut in enumerate(cuts):
            out = dot3(left, split2(dot3(split2(out_ref[rows, cut]), right[c])))
            out_ref[rows, cut] = out
            square = (out * out).reshape(BLK // 8, 8, BLK).sum(axis=0)
            for k in range(BLK // 128):
                total = total + square[:, k * 128 : (k + 1) * 128]
    sum_ref[...] = total


def scale_kernel(count, norm_ref, one_ref, two_ref, out_ref):
    total = jnp.sum(jnp.sum(norm_ref[...], axis=0, keepdims=True), axis=1, keepdims=True)
    scale = lax.rsqrt(total / count + 1e-06)
    out_ref[0] = (one_ref[...] * scale).astype(BF)
    out_ref[1] = (two_ref[...] * scale).astype(BF)


SIDE = 4


def send(array, by, inner):
    pairs = []
    for at in range(SIDE * SIDE):
        out, inn = at // SIDE, at % SIDE
        if inner:
            pairs.append((at, out * SIDE + (inn + by) % SIDE))
        else:
            pairs.append((at, (out + by) % SIDE * SIDE + inn))
    return lax.ppermute(array, "shard", pairs)


def gather(array, inner):
    line = jnp.concatenate([array] + [send(array, k, inner) for k in range(1, SIDE)], 0)
    half = line.shape[0] // 2
    before, after = send(line, 1, not inner), send(line, SIDE - 1, not inner)
    far = [send(before[:half], 1, not inner), send(after[half:], SIDE - 1, not inner)]
    return [line, before, *far, after]


def full(shape):
    return pl.BlockSpec(shape, lambda *_: (0,) * len(shape))


def local(tokens_in, out_grad, expert_ids, d_levels, f_levels):
    groups, shards = lax.axis_size("expert"), lax.axis_size("shard")
    toks, width = tokens_in.shape
    ff = out_grad.shape[2]
    ff_dev = ff // shards
    cap = min(toks, max(2, 5 * toks // (2 * groups)))
    live = groups * cap
    parts = 4
    ng = ff_dev // 128
    rows = -(-(ng * cap + 1) // 16) * 16
    vm, sm = pl.BlockSpec(memory_space=pltpu.VMEM), pl.BlockSpec(memory_space=pltpu.SMEM)

    def call(kernel, mib=16, **kwargs):
        params = pltpu.CompilerParams(vmem_limit_bytes=mib << 20)
        return pl.pallas_call(kernel, compiler_params=params, **kwargs)

    id_row = expert_ids.reshape(1, 2 * toks)
    id_col = expert_ids.reshape(2 * toks, 1)
    first, second = expert_ids[:, 0].reshape(1, toks), expert_ids[:, 1].reshape(1, toks)

    x_send = call(
        functools.partial(send_x_kernel, cap, parts),
        out_shape=jax.ShapeDtypeStruct((groups * cap * parts, width // parts), BF),
        name="send_x",
    )(id_col, first, second, tokens_in)
    x_recv = lax.all_to_all(
        x_send.reshape(groups, cap * parts, width // parts), "expert", 0, 0, tiled=True
    )
    x_one, x_two, x_three = call(
        functools.partial(take_x_kernel, cap, parts),
        out_shape=[
            jax.ShapeDtypeStruct((live, width // 2), BF),
            jax.ShapeDtypeStruct((live, width // 4), BF),
            jax.ShapeDtypeStruct((live, width // 4), BF),
        ],
        name="take_x",
    )(x_recv)
    x_one = [lax.all_gather(x_one, "shard", axis=0, tiled=True)]
    x_two, x_three = gather(x_two, True), gather(x_three, False)

    payload = call(
        functools.partial(payload_kernel, cap, rows, ng),
        out_shape=jax.ShapeDtypeStruct((shards, groups, rows, 128), BF),
        grid=(shards // 2,),
        in_specs=[
            full((2 * toks, 1)),
            full((1, 2 * toks)),
            pl.BlockSpec((2 * toks, 2 * ff_dev), lambda s: (0, s)),
        ],
        out_specs=pl.BlockSpec((2, groups, rows, 128), lambda s: (s, 0, 0, 0)),
        scratch_shapes=[
            pltpu.VMEM((groups * rows, ng * 2 * toks), BF),
            pltpu.VMEM((groups * rows, 1), F32),
        ],
        name="payload",
    )(id_col, id_row, out_grad.reshape(2 * toks, ff))
    received = lax.all_to_all(
        payload.reshape(shards * groups, rows, 128), ("shard", "expert"), 0, 0, tiled=True
    ).reshape(shards, groups, rows, 128)

    me = lax.axis_index("shard")
    order = jnp.arange(shards, dtype=jnp.int32)
    back_out = (me // SIDE - order // SIDE) % SIDE
    back_in = (me % SIDE - order % SIDE) % SIDE
    place = jnp.concatenate([back_out * SIDE + back_in, back_in * SIDE + back_out])
    *rows_g, count = call(
        functools.partial(rows_kernel, cap, ng),
        out_shape=[jax.ShapeDtypeStruct((shards, live, ff_dev), BF)] * 3
        + [jax.ShapeDtypeStruct((1, 128), F32)],
        in_specs=[sm, vm],
        out_specs=(vm,) * 4,
        name="rows",
    )(place, received)

    blocks = width // BLK // 2
    hidden = ff_dev // BLK
    levels = d_levels[0].astype(F32)
    precond = jax.ShapeDtypeStruct((width // 2, ff_dev), F32)
    partial = jax.ShapeDtypeStruct((8, 128), F32)
    one, square, inv_f = call(
        functools.partial(chunk_kernel, (1,), True),
        mib=36,
        out_shape=(precond, partial, jax.ShapeDtypeStruct((hidden, BLK, BLK), F32)),
        in_specs=[sm] + [vm] * 3,
        out_specs=(vm,) * 3,
        scratch_shapes=[pltpu.VMEM((blocks + hidden, BLK, BLK), F32)],
        name="first",
    )(jnp.concatenate([levels[:blocks], f_levels[0].astype(F32)]), count, *x_one, rows_g[0])
    two, square_two = call(
        functools.partial(chunk_kernel, (len(x_two), len(x_three)), False),
        mib=36,
        out_shape=(precond, partial),
        in_specs=[sm] + [vm] * (4 + len(x_two) + len(x_three)),
        out_specs=(vm,) * 2,
        scratch_shapes=[pltpu.VMEM((blocks, BLK, BLK), F32)],
        name="second",
    )(levels[blocks:], count, *x_two, *x_three, *rows_g[1:], inv_f)
    square = square + square_two

    norm = jnp.sum(square, axis=0, keepdims=True)
    norm = lax.all_to_all(jnp.broadcast_to(norm, (groups, 128)), "expert", 0, 0, tiled=True)
    norm = jnp.sum(norm, axis=0, keepdims=True)
    norm = lax.all_to_all(jnp.broadcast_to(norm, (shards, 128)), "shard", 0, 0, tiled=True)
    tile = width // 8
    ascent = call(
        functools.partial(scale_kernel, float(groups * width * ff)),
        out_shape=jax.ShapeDtypeStruct((2, width // 2, ff_dev), BF),
        grid=(4,),
        in_specs=[full((shards, 128))]
        + [pl.BlockSpec((tile, ff_dev), lambda i: (i, 0))] * 2,
        out_specs=pl.BlockSpec((2, tile, ff_dev), lambda i: (0, i, 0)),
        name="scale",
    )(norm, one, two)
    return ascent.reshape(1, width, ff_dev)


def solution(mesh):
    return jax.shard_map(
        local,
        mesh=mesh,
        in_specs=(
            P(("expert", "shard"), None),
            P(("expert", "shard"), None, None),
            P(("expert", "shard"), None),
            P("expert", None),
            P("expert", "shard"),
        ),
        out_specs=P("expert", None, "shard"),
        check_vma=False,
    )
```

```python
import functools

import jax
import jax.numpy as jnp
from jax import lax
from jax.experimental import pallas as pl
from jax.experimental.pallas import tpu as pltpu
from jax.sharding import PartitionSpec as P

BLK = 256
BASE = 32
PANEL = 8
F32 = jnp.float32
BF = jnp.bfloat16
TN = (((0,), (0,)), ((), ()))


def iota(shape, dim):
    return lax.broadcasted_iota(jnp.int32, shape, dim)


def div(value, by):
    return (value * (65536 // by + 1)) >> 16


def onehot(hit):
    return jnp.where(hit, 1.0, 0.0).astype(BF)


def split2(x):
    high = x.astype(BF)
    return high, (x - high.astype(F32)).astype(BF)


def split3(x):
    high = x.astype(BF)
    rest = x - high.astype(F32)
    mid = rest.astype(BF)
    return high, mid, (rest - mid.astype(F32)).astype(BF)


def tn_full(a, b):
    ah, am, al = split3(a)
    bh, bm, bl = split3(b)
    return lax.dot_general(
        jnp.concatenate([ah, ah, am, ah, al, am], 0),
        jnp.concatenate([bh, bm, bh, bl, bh, bm], 0),
        TN,
        preferred_element_type=F32,
    )


def dot3(a, b):
    ah, al = a
    bh, bl = b
    return jnp.dot(
        jnp.concatenate([ah, ah, al], 1),
        jnp.concatenate([bh, bl, bh], 0),
        preferred_element_type=F32,
    )


def invert_base(packs):
    lane, sub = iota((BASE, 128), 1), iota((BASE, 128), 0)
    start = (lane // BASE) * BASE
    inner = lane - start
    packs = list(packs)
    for k0 in range(0, BASE, PANEL):
        cols = [
            [jnp.take_along_axis(x, start + (k0 + j), axis=1) for j in range(PANEL)] for x in packs
        ]
        for j in range(PANEL):
            k = k0 + j
            is_col, is_row = inner == k, sub == k
            for g, x in enumerate(packs):
                col = cols[g][j]
                inv = 1.0 / col[k : k + 1, :]
                row = jnp.where(is_col[:1], 1.0, x[k : k + 1, :]) * inv
                for jj in range(j + 1, PANEL):
                    other = cols[g][jj]
                    scaled = other[k : k + 1, :] * inv
                    cols[g][jj] = jnp.where(is_row, scaled, other - col * scaled)
                packs[g] = jnp.where(is_row, row, jnp.where(is_col, 0.0, x) - col * row)
    return packs


def invert_all(m_ref, count):
    per = 128 // BASE
    lane, sub = iota((BASE, BLK), 1), iota((BASE, BLK), 0)
    wide = iota((BLK, BLK), 1)
    for low in range(0, BLK, BASE):
        end = low + BASE
        packs = [
            jnp.concatenate(
                [m_ref[min(g + j, count - 1), low:end, low:end] for j in range(per)], axis=1
            )
            for g in range(0, count, per)
        ]
        packs = invert_base(packs)
        own = (lane >= low) & (lane < end)
        minus_eye = jnp.where(lane - low == sub, -1.0, 0.0)
        for m in range(count):
            at = (m % per) * BASE
            pivot = packs[m // per][:, at : at + BASE]
            rows = m_ref[m, low:end, :]
            new_rows = tn_full(pivot, jnp.where(own, minus_eye, rows))
            change = tn_full(jnp.where(own, 0.0, rows), new_rows)
            m_ref[m] = jnp.where((wide >= low) & (wide < end), 0.0, m_ref[m]) - change
            m_ref[m, low:end, :] = new_rows


def slots(id_col, id_row, first, step, capacity):
    shape = (id_col.shape[0], id_row.shape[1])
    earlier = iota(shape, 0) < first + step * iota(shape, 1)
    same = (id_col == id_row) & earlier
    rank = jnp.sum(jnp.where(same, 1, 0), axis=0, keepdims=True)
    return id_row, rank


def send_x_kernel(cap, parts, per, col_ref, row_ref, first_ref, second_ref, x_ref, out_ref):
    rows, toks = out_ref.shape[0], x_ref.shape[0]
    width = out_ref.shape[1]
    hot = []
    row = iota((rows, toks), 0)
    for part in range(parts):
        total = None
        for j, ids in enumerate((first_ref, second_ref)):
            expert, rank = slots(col_ref[...], ids[...], j, 2, cap)
            hit = jnp.where(row == expert * per + part * cap + rank, 1.0, 0.0)
            total = hit if total is None else total + hit
        hot.append(total.astype(BF))
    data = jnp.concatenate([x_ref[:, p * width : (p + 1) * width] for p in range(parts)], 0)
    out = jnp.dot(jnp.concatenate(hot, 1), data, preferred_element_type=F32)
    pairs = row_ref.shape[1]
    mark = iota((rows, pairs), 0) == row_ref[...] * per + parts * cap
    out = out + jnp.sum(jnp.where(mark, 1.0, 0.0), axis=1, keepdims=True)
    out_ref[...] = out.astype(BF)


def take_x_kernel(cap, parts, in_ref, one_ref, two_ref, own_ref):
    groups, per, width = in_ref.shape
    live = groups * cap
    data = in_ref[...].reshape(groups * per, width)
    shape = (live, groups * per)
    row = iota(shape, 0)
    source = div(row, cap)
    base = source * per + (row - source * cap)
    half = parts // 2
    count = jnp.zeros((1, width), F32)
    for g in range(groups):
        count = count + in_ref[g, parts * cap : parts * cap + 1, :].astype(F32)
    mark = jnp.broadcast_to(count, (own_ref.shape[1] - live, width)).astype(BF)
    for part in range(parts):
        pick = onehot(iota(shape, 1) == base + part * cap)
        got = jnp.dot(pick, data, preferred_element_type=F32).astype(BF)
        at = part % half * width
        (two_ref if part >= half else one_ref)[:, at : at + width] = got
        own_ref[part, :live] = got
        own_ref[part, live:] = mark


def payload_kernel(cap, rows, ng, col_ref, row_ref, g_ref, out_ref, hot_ref):
    pair, groups = out_ref.shape[:2]
    pairs = g_ref.shape[0]
    total = groups * rows

    @pl.when(pl.program_id(0) == 0)
    def _():
        expert, rank = slots(col_ref[...], row_ref[...], 0, 1, cap)
        row = iota((total, pairs), 0)
        for part in range(ng):
            target = expert * rows + part * cap + rank
            hot_ref[:, part * pairs : (part + 1) * pairs] = onehot(row == target)

    data = jnp.concatenate(
        [
            jnp.concatenate(
                [g_ref[:, (t * ng + p) * 128 : (t * ng + p + 1) * 128] for t in range(pair)], 1
            )
            for p in range(ng)
        ],
        0,
    )
    out = jnp.dot(hot_ref[...], data, preferred_element_type=F32)
    for t in range(pair):
        piece = out[:, t * 128 : (t + 1) * 128].astype(BF)
        out_ref[t] = piece.reshape(groups, rows, 128)


def damped(cov, count, level):
    eye = iota((BLK, BLK), 0) == iota((BLK, BLK), 1)
    damp = 0.05 * jnp.exp(0.4 * jnp.full((1, 1), level, F32))
    return cov / count + jnp.where(eye, damp, 0.0)


def input_kernel(live, lev_ref, in_ref, out_ref, count_ref, m_ref):
    shards, rows, _ = in_ref.shape
    total = jnp.zeros((1, 128), F32)
    for s in range(shards):
        total = total + in_ref[s, live : live + 1, :128].astype(F32)
    count_ref[...] = total
    x = jnp.concatenate([in_ref[s, :live] for s in range(shards)], 0)
    cov = lax.dot_general(x, x, TN, preferred_element_type=F32)
    m_ref[0] = damped(cov, total[:, :1], lev_ref[0])
    invert_all(m_ref, 1)
    half = BLK // 2
    top, low = -m_ref[0, :half, :half], -m_ref[0, half:, half:]
    down, across = iota((half, half), 0), iota((half, half), 1)
    diag = jnp.sum(jnp.where(down == across, low, 0.0), axis=0, keepdims=True)
    out_ref[:half] = -m_ref[0, :half, half:]
    out_ref[half : 2 * half] = jnp.where(down >= across, top, low)
    out_ref[2 * half :] = jnp.broadcast_to(diag, (8, half))


def unfold(ref):
    half = ref.shape[1]
    quarter, both, diag = ref[:half], ref[half : 2 * half], ref[2 * half : 2 * half + 1]
    down, across = iota((half, half), 0), iota((half, half), 1)
    lower = jnp.where(down > across, both, 0.0)
    upper = jnp.where(down < across, both, 0.0)
    eye = down == across
    top = lower + lower.T + jnp.where(eye, both, 0.0)
    low = upper + upper.T + jnp.where(eye, diag, 0.0)
    return jnp.concatenate(
        [jnp.concatenate([top, quarter], 1), jnp.concatenate([quarter.T, low], 1)], 0
    )


def hidden_kernel(cap, ng, rel_ref, lev_ref, count_ref, in_ref, one_ref, two_ref, s_ref, m_ref):
    shards, groups, rows, _ = in_ref.shape
    live = groups * cap
    shape = (live, groups * rows)
    row = iota(shape, 0)
    source = div(row, cap)
    base = source * rows + (row - source * cap)
    pick = jnp.concatenate([onehot(iota(shape, 1) == base + p * cap) for p in range(ng)], 0)
    for s in range(shards):
        data = in_ref[s].reshape(groups * rows, 128)
        got = jnp.dot(pick, data, preferred_element_type=F32).astype(BF)
        h = jnp.concatenate([got[p * live : (p + 1) * live] for p in range(ng)], 1)
        one_ref[rel_ref[s]] = h
        two_ref[rel_ref[shards + s]] = h
    h = one_ref[...].reshape(shards * live, -1)
    for c in range(m_ref.shape[0]):
        part = h[:, c * BLK : (c + 1) * BLK]
        cov = lax.dot_general(part, part, TN, preferred_element_type=F32)
        m_ref[c] = damped(cov, count_ref[:, :1], lev_ref[c])
    invert_all(m_ref, m_ref.shape[0])
    s_ref[...] = -m_ref[...]


def product_kernel(pieces, *refs):
    x_refs, refs = (refs[:pieces], refs[pieces : 2 * pieces]), refs[2 * pieces :]
    h_refs, a_refs, s_ref, out_refs, sum_ref = refs[0:2], refs[2:4], refs[4], refs[5:7], refs[7]
    width = h_refs[0].shape[2]
    right = [split2(s_ref[c]) for c in range(width // BLK)]
    total = jnp.zeros((8, 128), F32)
    for half in range(2):
        x = jnp.concatenate([ref[...] for ref in x_refs[half]], 0)
        h = h_refs[half][...].reshape(x.shape[0], width)
        gradient = lax.dot_general(x, h, TN, preferred_element_type=F32)
        left = split2(unfold(a_refs[half]))
        for c in range(width // BLK):
            cut = slice(c * BLK, (c + 1) * BLK)
            out = dot3(left, split2(dot3(split2(gradient[:, cut]), right[c])))
            out_refs[half][:, cut] = out
            square = (out * out).reshape(BLK // 8, 8, BLK).sum(axis=0)
            for k in range(BLK // 128):
                total = total + square[:, k * 128 : (k + 1) * 128]

    @pl.when(pl.program_id(0) == 0)
    def _():
        sum_ref[...] = jnp.zeros_like(sum_ref)

    sum_ref[...] += total


def scale_kernel(count, norm_ref, one_ref, two_ref, out_ref):
    total = jnp.sum(jnp.sum(norm_ref[...], axis=0, keepdims=True), axis=1, keepdims=True)
    scale = lax.rsqrt(total / count + 1e-06)
    out_ref[0] = (one_ref[...] * scale).astype(BF)
    out_ref[1] = (two_ref[...] * scale).astype(BF)


SIDE = 4


def send(array, by, inner):
    pairs = []
    for at in range(SIDE * SIDE):
        out, inn = at // SIDE, at % SIDE
        if inner:
            pairs.append((at, out * SIDE + (inn + by) % SIDE))
        else:
            pairs.append((at, (out + by) % SIDE * SIDE + inn))
    return lax.ppermute(array, "shard", pairs)


def gather(one, two, other):
    sides = range(1, SIDE)
    first = [send(one, k, True) for k in sides], [send(two, k, False) for k in sides]
    *first, other = lax.optimization_barrier((*first, other))
    lines = [jnp.concatenate([array, *got], 0) for array, got in zip((one, two), first)]
    half = lines[0].shape[0] // 2
    pieces = []
    for line, inner in zip(lines, (False, True)):
        before, after = send(line, 1, inner), send(line, SIDE - 1, inner)
        far = [send(before[:half], 1, inner), send(after[half:], SIDE - 1, inner)]
        pieces.append([line, before, *far, after])
    return *pieces, other


def in_hbm(*arrays):
    return [pltpu.with_memory_space_constraint(array, pltpu.HBM) for array in arrays]


def full(shape):
    return pl.BlockSpec(shape, lambda *_: (0,) * len(shape))


def local(tokens_in, out_grad, expert_ids, d_levels, f_levels):
    groups, shards = lax.axis_size("expert"), lax.axis_size("shard")
    toks, width = tokens_in.shape
    ff = out_grad.shape[2]
    ff_dev = ff // shards
    cap = min(toks, max(2, 5 * toks // (2 * groups)))
    live = groups * cap
    own = width // shards
    ng = ff_dev // 128
    per = shards * cap + 8
    vm, sm = pl.BlockSpec(memory_space=pltpu.VMEM), pl.BlockSpec(memory_space=pltpu.SMEM)

    def call(kernel, micros, mib=16, **kwargs):
        params = pltpu.CompilerParams(vmem_limit_bytes=mib << 20)
        cost = pl.CostEstimate(
            flops=micros * 1_000_000_000, transcendentals=0, bytes_accessed=micros * 1_000_000
        )
        return pl.pallas_call(kernel, compiler_params=params, cost_estimate=cost, **kwargs)

    id_row = expert_ids.reshape(1, 2 * toks)
    id_col = expert_ids.reshape(2 * toks, 1)
    first, second = expert_ids[:, 0].reshape(1, toks), expert_ids[:, 1].reshape(1, toks)

    x_send = call(
        functools.partial(send_x_kernel, cap, shards, per),
        3,
        out_shape=jax.ShapeDtypeStruct((groups * per, own), BF),
        name="send_x",
    )(id_col, id_row, first, second, tokens_in)
    x_recv = lax.all_to_all(x_send.reshape(groups, per, own), "expert", 0, 0, tiled=True)
    x_one, x_two, x_own = call(
        functools.partial(take_x_kernel, cap, shards),
        3,
        out_shape=[
            jax.ShapeDtypeStruct((live, width // 2), BF),
            jax.ShapeDtypeStruct((live, width // 2), BF),
            jax.ShapeDtypeStruct((shards, live + 8, own), BF),
        ],
        name="take_x",
    )(x_recv)
    x_own = lax.all_to_all(x_own, "shard", 0, 0, tiled=True)
    x_one, x_two, x_own = gather(x_one, x_two, x_own)

    me = lax.axis_index("shard")
    folded, count = call(
        functools.partial(input_kernel, live),
        13,
        out_shape=[
            jax.ShapeDtypeStruct((BLK + 8, BLK // 2), F32),
            jax.ShapeDtypeStruct((1, 128), F32),
        ],
        in_specs=[sm, vm],
        out_specs=(vm, vm),
        scratch_shapes=[pltpu.VMEM((1, BLK, BLK), F32)],
        name="input",
    )(lax.dynamic_slice_in_dim(d_levels[0], me, 1, 0).astype(F32), x_own)
    folded = lax.all_gather(folded, "shard", axis=0, tiled=True)

    rows = ng * cap
    payload = call(
        functools.partial(payload_kernel, cap, rows, ng),
        4,
        out_shape=jax.ShapeDtypeStruct((shards, groups, rows, 128), BF),
        grid=(shards // 2,),
        in_specs=[
            full((2 * toks, 1)),
            full((1, 2 * toks)),
            pl.BlockSpec((2 * toks, 2 * ff_dev), lambda s: (0, s)),
        ],
        out_specs=pl.BlockSpec((2, groups, rows, 128), lambda s: (s, 0, 0, 0)),
        scratch_shapes=[
            pltpu.VMEM((groups * rows, ng * 2 * toks), BF),
        ],
        name="payload",
    )(id_col, id_row, out_grad.reshape(2 * toks, ff))
    received = lax.all_to_all(
        payload.reshape(shards * groups, rows, 128), ("shard", "expert"), 0, 0, tiled=True
    ).reshape(shards, groups, rows, 128)

    order = jnp.arange(shards, dtype=jnp.int32)
    back_out = (me // SIDE - order // SIDE) % SIDE
    back_in = (me % SIDE - order % SIDE) % SIDE
    place = jnp.concatenate([back_out * SIDE + back_in, back_in * SIDE + back_out])
    hidden = ff_dev // BLK
    *rows_g, inv_f = call(
        functools.partial(hidden_kernel, cap, ng),
        16,
        out_shape=[pltpu.HBM((shards, live, ff_dev), BF)] * 2
        + [pltpu.HBM((hidden, BLK, BLK), F32)],
        in_specs=[sm, sm, vm, vm],
        out_specs=(vm,) * 3,
        scratch_shapes=[pltpu.VMEM((hidden, BLK, BLK), F32)],
        name="hidden",
    )(place, f_levels[0].astype(F32), count, received)

    steps = shards // 2

    def columns(pieces):
        return [pl.BlockSpec((p.shape[0], BLK), lambda i: (0, i)) for p in pieces]

    one, two, square = call(
        functools.partial(product_kernel, len(x_one)),
        14,
        out_shape=(
            pltpu.HBM((width // 2, ff_dev), F32),
            pltpu.HBM((width // 2, ff_dev), F32),
            jax.ShapeDtypeStruct((8, 128), F32),
        ),
        grid=(steps,),
        in_specs=[
            *columns(x_one),
            *columns(x_two),
            full((shards, live, ff_dev)),
            full((shards, live, ff_dev)),
            pl.BlockSpec((BLK + 8, BLK // 2), lambda i: (i, 0)),
            pl.BlockSpec((BLK + 8, BLK // 2), lambda i: (steps + i, 0)),
            full((hidden, BLK, BLK)),
        ],
        out_specs=(
            pl.BlockSpec((BLK, ff_dev), lambda i: (i, 0)),
            pl.BlockSpec((BLK, ff_dev), lambda i: (i, 0)),
            full((8, 128)),
        ),
        name="product",
    )(*in_hbm(*x_one, *x_two, *rows_g, folded, folded, inv_f))

    norm = jnp.sum(square, axis=0, keepdims=True)
    norm = lax.all_to_all(jnp.broadcast_to(norm, (groups, 128)), "expert", 0, 0, tiled=True)
    norm = jnp.sum(norm, axis=0, keepdims=True)
    norm = lax.all_to_all(jnp.broadcast_to(norm, (shards, 128)), "shard", 0, 0, tiled=True)
    tile = width // 8
    ascent = call(
        functools.partial(scale_kernel, float(groups * width * ff)),
        3,
        out_shape=jax.ShapeDtypeStruct((2, width // 2, ff_dev), BF),
        grid=(4,),
        in_specs=[full((shards, 128))]
        + [pl.BlockSpec((tile, ff_dev), lambda i: (i, 0))] * 2,
        out_specs=pl.BlockSpec((2, tile, ff_dev), lambda i: (0, i, 0)),
        name="scale",
    )(norm, *in_hbm(one, two))
    return ascent.reshape(1, width, ff_dev)


def solution(mesh):
    return jax.shard_map(
        local,
        mesh=mesh,
        in_specs=(
            P(("expert", "shard"), None),
            P(("expert", "shard"), None, None),
            P(("expert", "shard"), None),
            P("expert", None),
            P("expert", "shard"),
        ),
        out_specs=P("expert", None, "shard"),
        check_vma=False,
    )
```

```python
import functools

import jax
import jax.numpy as jnp
from jax import lax
from jax.experimental import pallas as pl
from jax.experimental.pallas import tpu as pltpu
from jax.sharding import PartitionSpec as P

BLK = 256
BASE = 32
PANEL = 8
F32 = jnp.float32
BF = jnp.bfloat16
TN = (((0,), (0,)), ((), ()))


def iota(shape, dim):
    return lax.broadcasted_iota(jnp.int32, shape, dim)


def div(value, by):
    return (value * (65536 // by + 1)) >> 16


def onehot(hit):
    return jnp.where(hit, 1.0, 0.0).astype(BF)


def split2(x):
    high = x.astype(BF)
    return high, (x - high.astype(F32)).astype(BF)


def split3(x):
    high = x.astype(BF)
    rest = x - high.astype(F32)
    mid = rest.astype(BF)
    return high, mid, (rest - mid.astype(F32)).astype(BF)


def tn_full(a, b):
    ah, am, al = split3(a)
    bh, bm, bl = split3(b)
    return lax.dot_general(
        jnp.concatenate([ah, ah, am, ah, al, am], 0),
        jnp.concatenate([bh, bm, bh, bl, bh, bm], 0),
        TN,
        preferred_element_type=F32,
    )


def dot3(a, b):
    ah, al = a
    bh, bl = b
    return jnp.dot(
        jnp.concatenate([ah, ah, al], 1),
        jnp.concatenate([bh, bl, bh], 0),
        preferred_element_type=F32,
    )


def invert_base(packs):
    lane, sub = iota((BASE, 128), 1), iota((BASE, 128), 0)
    start = (lane // BASE) * BASE
    inner = lane - start
    packs = list(packs)
    for k0 in range(0, BASE, PANEL):
        cols = [
            [jnp.take_along_axis(x, start + (k0 + j), axis=1) for j in range(PANEL)] for x in packs
        ]
        for j in range(PANEL):
            k = k0 + j
            is_col, is_row = inner == k, sub == k
            for g, x in enumerate(packs):
                col = cols[g][j]
                inv = 1.0 / col[k : k + 1, :]
                row = jnp.where(is_col[:1], 1.0, x[k : k + 1, :]) * inv
                for jj in range(j + 1, PANEL):
                    other = cols[g][jj]
                    scaled = other[k : k + 1, :] * inv
                    cols[g][jj] = jnp.where(is_row, scaled, other - col * scaled)
                packs[g] = jnp.where(is_row, row, jnp.where(is_col, 0.0, x) - col * row)
    return packs


def invert_all(m_ref, count):
    per = 128 // BASE
    lane, sub = iota((BASE, BLK), 1), iota((BASE, BLK), 0)
    wide = iota((BLK, BLK), 1)
    for low in range(0, BLK, BASE):
        end = low + BASE
        packs = [
            jnp.concatenate(
                [m_ref[min(g + j, count - 1), low:end, low:end] for j in range(per)], axis=1
            )
            for g in range(0, count, per)
        ]
        packs = invert_base(packs)
        own = (lane >= low) & (lane < end)
        minus_eye = jnp.where(lane - low == sub, -1.0, 0.0)
        for m in range(count):
            at = (m % per) * BASE
            pivot = packs[m // per][:, at : at + BASE]
            rows = m_ref[m, low:end, :]
            new_rows = tn_full(pivot, jnp.where(own, minus_eye, rows))
            change = tn_full(jnp.where(own, 0.0, rows), new_rows)
            m_ref[m] = jnp.where((wide >= low) & (wide < end), 0.0, m_ref[m]) - change
            m_ref[m, low:end, :] = new_rows


def slots(id_col, id_row, first, step, capacity):
    shape = (id_col.shape[0], id_row.shape[1])
    earlier = iota(shape, 0) < first + step * iota(shape, 1)
    same = (id_col == id_row) & earlier
    rank = jnp.sum(jnp.where(same, 1, 0), axis=0, keepdims=True)
    return id_row, rank


def send_x_kernel(cap, parts, col_ref, first_ref, second_ref, x_ref, out_ref):
    rows, toks = out_ref.shape[0], x_ref.shape[0]
    width = x_ref.shape[1] // parts
    per = cap * parts
    hot = []
    for part in range(parts):
        total = None
        for j, ids in enumerate((first_ref, second_ref)):
            expert, rank = slots(col_ref[...], ids[...], j, 2, cap)
            target = expert * per + part * cap + rank
            hit = jnp.where(iota((rows, toks), 0) == target, 1.0, 0.0)
            total = hit if total is None else total + hit
        hot.append(total.astype(BF))
    data = jnp.concatenate([x_ref[:, p * width : (p + 1) * width] for p in range(parts)], 0)
    out_ref[...] = jnp.dot(
        jnp.concatenate(hot, 1), data, preferred_element_type=F32
    ).astype(BF)


def take_x_kernel(cap, parts, in_ref, *out_refs):
    groups, per, width = in_ref.shape
    data = in_ref[...].reshape(groups * per, width)
    shape = (groups * cap, groups * per)
    row = iota(shape, 0)
    source = div(row, cap)
    base = source * per + (row - source * cap)
    for part in range(parts):
        pick = onehot(iota(shape, 1) == base + part * cap)
        rest = part * width
        got = jnp.dot(pick, data, preferred_element_type=F32).astype(BF)
        for ref in out_refs:
            if 0 <= rest < ref.shape[1]:
                ref[:, rest : rest + width] = got
            rest -= ref.shape[1]


def payload_kernel(cap, rows, ng, col_ref, row_ref, g_ref, out_ref, hot_ref, add_ref):
    pair, groups = out_ref.shape[:2]
    pairs = g_ref.shape[0]
    total = groups * rows

    @pl.when(pl.program_id(0) == 0)
    def _():
        expert, rank = slots(col_ref[...], row_ref[...], 0, 1, cap)
        row = iota((total, pairs), 0)
        for part in range(ng):
            target = expert * rows + part * cap + rank
            hot_ref[:, part * pairs : (part + 1) * pairs] = onehot(row == target)
        marked = row == row_ref[...] * rows + ng * cap
        add_ref[...] = jnp.sum(jnp.where(marked, 1.0, 0.0), axis=1, keepdims=True)

    data = jnp.concatenate(
        [
            jnp.concatenate(
                [g_ref[:, (t * ng + p) * 128 : (t * ng + p + 1) * 128] for t in range(pair)], 1
            )
            for p in range(ng)
        ],
        0,
    )
    out = jnp.dot(hot_ref[...], data, preferred_element_type=F32) + add_ref[...]
    for t in range(pair):
        piece = out[:, t * 128 : (t + 1) * 128].astype(BF)
        out_ref[t] = piece.reshape(groups, rows, 128)


def rows_kernel(cap, ng, rel_ref, in_ref, one_ref, two_ref, count_ref):
    shards, groups, rows, _ = in_ref.shape
    live = groups * cap
    shape = (live, groups * rows)
    row = iota(shape, 0)
    source = div(row, cap)
    base = source * rows + (row - source * cap)
    pick = jnp.concatenate([onehot(iota(shape, 1) == base + p * cap) for p in range(ng)], 0)
    total = jnp.zeros((1, 128), F32)
    for s in range(shards):
        data = in_ref[s].reshape(groups * rows, 128)
        got = jnp.dot(pick, data, preferred_element_type=F32).astype(BF)
        h = jnp.concatenate([got[p * live : (p + 1) * live] for p in range(ng)], 1)
        one_ref[rel_ref[s]] = h
        two_ref[rel_ref[shards + s]] = h
        for g in range(groups):
            total = total + in_ref[s, g, ng * cap : ng * cap + 1, :].astype(F32)
    count_ref[...] = total


def solve_kernel(pieces, lev_ref, count_ref, *refs):
    x_refs, refs = (refs[:pieces], refs[pieces : 2 * pieces]), refs[2 * pieces :]
    h_refs, (out_ref, sum_ref, m_ref, g_ref, sem_ref) = refs[:2], refs[2:]
    width = g_ref.shape[2]
    cuts = [slice(c * BLK, (c + 1) * BLK) for c in range(width // BLK)]
    scale = 1.0 / count_ref[:, :1]
    eye = iota((BLK, BLK), 0) == iota((BLK, BLK), 1)

    def set_block(at, cov):
        damp = 0.05 * jnp.exp(0.4 * jnp.full((1, 1), lev_ref[at], F32))
        m_ref[at] = cov * scale + jnp.where(eye, damp, 0.0)

    block = 0
    for x_pieces, h_ref in zip(x_refs, h_refs):
        h = h_ref[...].reshape(-1, width)
        for at in range(0, x_pieces[0].shape[1], BLK):
            x = jnp.concatenate([ref[:, at : at + BLK] for ref in x_pieces], 0)
            both = lax.dot_general(
                x, jnp.concatenate([x, h], 1), TN, preferred_element_type=F32
            )
            set_block(block, both[:, :BLK])
            g_ref[block] = both[:, BLK:]
            block += 1
    h = h_refs[0][...].reshape(-1, width)
    for c, cut in enumerate(cuts):
        part = h[:, cut]
        set_block(block + c, lax.dot_general(part, part, TN, preferred_element_type=F32))
    invert_all(m_ref, m_ref.shape[0])
    right = [split2(-m_ref[block + c]) for c in range(len(cuts))]
    total = jnp.zeros((8, 128), F32)

    def copy(b):
        return pltpu.make_async_copy(g_ref.at[b], out_ref.at[b], sem_ref.at[b])

    for b in range(block):
        left = split2(-m_ref[b])
        for c, cut in enumerate(cuts):
            out = dot3(left, split2(dot3(split2(g_ref[b, :, cut]), right[c])))
            g_ref[b, :, cut] = out
            square = (out * out).reshape(BLK // 8, 8, BLK).sum(axis=0)
            for k in range(BLK // 128):
                total = total + square[:, k * 128 : (k + 1) * 128]
        copy(b).start()
    sum_ref[...] = total
    for b in range(block):
        copy(b).wait()


def scale_kernel(count, norm_ref, in_ref, out_ref):
    total = jnp.sum(jnp.sum(norm_ref[...], axis=0, keepdims=True), axis=1, keepdims=True)
    out_ref[...] = (in_ref[...] * lax.rsqrt(total / count + 1e-06)).astype(BF)


SIDE = 4


def send(array, by, inner):
    pairs = []
    for at in range(SIDE * SIDE):
        out, inn = at // SIDE, at % SIDE
        if inner:
            pairs.append((at, out * SIDE + (inn + by) % SIDE))
        else:
            pairs.append((at, (out + by) % SIDE * SIDE + inn))
    return lax.ppermute(array, "shard", pairs)


def gather(one, two, other):
    sides = range(1, SIDE)
    first = [send(one, k, True) for k in sides], [send(two, k, False) for k in sides]
    *first, other = lax.optimization_barrier((*first, other))
    lines = [jnp.concatenate([array, *got], 0) for array, got in zip((one, two), first)]
    half = lines[0].shape[0] // 2
    pieces = []
    for line, inner in zip(lines, (False, True)):
        before, after = send(line, 1, inner), send(line, SIDE - 1, inner)
        far = [send(before[:half], 1, inner), send(after[half:], SIDE - 1, inner)]
        pieces.append([line, before, *far, after])
    return *pieces, other


def in_hbm(*arrays):
    return [pltpu.with_memory_space_constraint(array, pltpu.HBM) for array in arrays]


def full(shape):
    return pl.BlockSpec(shape, lambda *_: (0,) * len(shape))


def local(tokens_in, out_grad, expert_ids, d_levels, f_levels):
    groups, shards = lax.axis_size("expert"), lax.axis_size("shard")
    toks, width = tokens_in.shape
    ff = out_grad.shape[2]
    ff_dev = ff // shards
    cap = min(toks, max(2, 5 * toks // (2 * groups)))
    live = groups * cap
    parts = 4
    ng = ff_dev // 128
    rows = -(-(ng * cap + 1) // 16) * 16
    vm, sm = pl.BlockSpec(memory_space=pltpu.VMEM), pl.BlockSpec(memory_space=pltpu.SMEM)

    def call(kernel, mib=16, **kwargs):
        params = pltpu.CompilerParams(vmem_limit_bytes=mib << 20)
        return pl.pallas_call(kernel, compiler_params=params, **kwargs)

    id_row = expert_ids.reshape(1, 2 * toks)
    id_col = expert_ids.reshape(2 * toks, 1)
    first, second = expert_ids[:, 0].reshape(1, toks), expert_ids[:, 1].reshape(1, toks)

    x_send = call(
        functools.partial(send_x_kernel, cap, parts),
        out_shape=jax.ShapeDtypeStruct((groups * cap * parts, width // parts), BF),
        name="send_x",
    )(id_col, first, second, tokens_in)
    x_recv = lax.all_to_all(
        x_send.reshape(groups, cap * parts, width // parts), "expert", 0, 0, tiled=True
    )
    x_one, x_two = call(
        functools.partial(take_x_kernel, cap, parts),
        out_shape=[
            jax.ShapeDtypeStruct((live, width // 2), BF),
            jax.ShapeDtypeStruct((live, width // 2), BF),
        ],
        name="take_x",
    )(x_recv)
    payload = call(
        functools.partial(payload_kernel, cap, rows, ng),
        out_shape=jax.ShapeDtypeStruct((shards, groups, rows, 128), BF),
        grid=(shards // 2,),
        in_specs=[
            full((2 * toks, 1)),
            full((1, 2 * toks)),
            pl.BlockSpec((2 * toks, 2 * ff_dev), lambda s: (0, s)),
        ],
        out_specs=pl.BlockSpec((2, groups, rows, 128), lambda s: (s, 0, 0, 0)),
        scratch_shapes=[
            pltpu.VMEM((groups * rows, ng * 2 * toks), BF),
            pltpu.VMEM((groups * rows, 1), F32),
        ],
        name="payload",
    )(id_col, id_row, out_grad.reshape(2 * toks, ff))
    x_one, x_two, payload = gather(x_one, x_two, payload)
    received = lax.all_to_all(
        payload.reshape(shards * groups, rows, 128), ("shard", "expert"), 0, 0, tiled=True
    ).reshape(shards, groups, rows, 128)

    me = lax.axis_index("shard")
    order = jnp.arange(shards, dtype=jnp.int32)
    back_out = (me // SIDE - order // SIDE) % SIDE
    back_in = (me % SIDE - order % SIDE) % SIDE
    place = jnp.concatenate([back_out * SIDE + back_in, back_in * SIDE + back_out])
    *rows_g, count = call(
        functools.partial(rows_kernel, cap, ng),
        out_shape=[jax.ShapeDtypeStruct((shards, live, ff_dev), BF)] * 2
        + [jax.ShapeDtypeStruct((1, 128), F32)],
        in_specs=[sm, vm],
        out_specs=(vm,) * 3,
        name="rows",
    )(place, received)

    blocks = width // BLK
    total = blocks + ff_dev // BLK
    precond, square = call(
        functools.partial(solve_kernel, len(x_one)),
        mib=48,
        out_shape=(
            jax.ShapeDtypeStruct((blocks, BLK, ff_dev), F32),
            jax.ShapeDtypeStruct((8, 128), F32),
        ),
        in_specs=[sm] + [vm] * (3 + 2 * len(x_one)),
        out_specs=(pl.BlockSpec(memory_space=pl.ANY), vm),
        scratch_shapes=[
            pltpu.VMEM((total, BLK, BLK), F32),
            pltpu.VMEM((blocks, BLK, ff_dev), F32),
            pltpu.SemaphoreType.DMA((blocks,)),
        ],
        name="solve",
    )(jnp.concatenate([d_levels[0], f_levels[0]]).astype(F32), count, *x_one, *x_two, *rows_g)

    norm = jnp.sum(square, axis=0, keepdims=True)
    norm = lax.all_to_all(jnp.broadcast_to(norm, (groups, 128)), "expert", 0, 0, tiled=True)
    norm = jnp.sum(norm, axis=0, keepdims=True)
    norm = lax.all_to_all(jnp.broadcast_to(norm, (shards, 128)), "shard", 0, 0, tiled=True)
    tile = width // 8
    ascent = call(
        functools.partial(scale_kernel, float(groups * width * ff)),
        out_shape=jax.ShapeDtypeStruct((width, ff_dev), BF),
        grid=(8,),
        in_specs=[full((shards, 128)), pl.BlockSpec((tile, ff_dev), lambda i: (i, 0))],
        out_specs=pl.BlockSpec((tile, ff_dev), lambda i: (i, 0)),
        name="scale",
    )(norm, *in_hbm(precond.reshape(width, ff_dev)))
    return ascent[None]


def solution(mesh):
    return jax.shard_map(
        local,
        mesh=mesh,
        in_specs=(
            P(("expert", "shard"), None),
            P(("expert", "shard"), None, None),
            P(("expert", "shard"), None),
            P("expert", None),
            P("expert", "shard"),
        ),
        out_specs=P("expert", None, "shard"),
        check_vma=False,
    )
```

```python
import functools

import jax
import jax.numpy as jnp
from jax import lax
from jax.experimental import pallas as pl
from jax.experimental.pallas import tpu as pltpu
from jax.sharding import PartitionSpec as P

BLK = 256
BASE = 32
PANEL = 8
F32 = jnp.float32
BF = jnp.bfloat16
TN = (((0,), (0,)), ((), ()))


def iota(shape, dim):
    return lax.broadcasted_iota(jnp.int32, shape, dim)


def div(value, by):
    return (value * (65536 // by + 1)) >> 16


def onehot(hit):
    return jnp.where(hit, 1.0, 0.0).astype(BF)


def split2(x):
    high = x.astype(BF)
    return high, (x - high.astype(F32)).astype(BF)


def split3(x):
    high = x.astype(BF)
    rest = x - high.astype(F32)
    mid = rest.astype(BF)
    return high, mid, (rest - mid.astype(F32)).astype(BF)


def tn_full(a, b):
    ah, am, al = split3(a)
    bh, bm, bl = split3(b)
    return lax.dot_general(
        jnp.concatenate([ah, ah, am, ah, al, am], 0),
        jnp.concatenate([bh, bm, bh, bl, bh, bm], 0),
        TN,
        preferred_element_type=F32,
    )


def dot3(a, b):
    ah, al = a
    bh, bl = b
    return jnp.dot(
        jnp.concatenate([ah, ah, al], 1),
        jnp.concatenate([bh, bl, bh], 0),
        preferred_element_type=F32,
    )


def invert_base(packs):
    lane, sub = iota((BASE, 128), 1), iota((BASE, 128), 0)
    start = (lane // BASE) * BASE
    inner = lane - start
    packs = list(packs)
    for k0 in range(0, BASE, PANEL):
        cols = [
            [jnp.take_along_axis(x, start + (k0 + j), axis=1) for j in range(PANEL)] for x in packs
        ]
        for j in range(PANEL):
            k = k0 + j
            is_col, is_row = inner == k, sub == k
            for g, x in enumerate(packs):
                col = cols[g][j]
                inv = 1.0 / col[k : k + 1, :]
                row = jnp.where(is_col[:1], 1.0, x[k : k + 1, :]) * inv
                for jj in range(j + 1, PANEL):
                    other = cols[g][jj]
                    scaled = other[k : k + 1, :] * inv
                    cols[g][jj] = jnp.where(is_row, scaled, other - col * scaled)
                packs[g] = jnp.where(is_row, row, jnp.where(is_col, 0.0, x) - col * row)
    return packs


def invert_all(m_ref, count):
    per = 128 // BASE
    lane, sub = iota((BASE, BLK), 1), iota((BASE, BLK), 0)
    wide = iota((BLK, BLK), 1)
    for low in range(0, BLK, BASE):
        end = low + BASE
        packs = [
            jnp.concatenate(
                [m_ref[min(g + j, count - 1), low:end, low:end] for j in range(per)], axis=1
            )
            for g in range(0, count, per)
        ]
        packs = invert_base(packs)
        own = (lane >= low) & (lane < end)
        minus_eye = jnp.where(lane - low == sub, -1.0, 0.0)
        for m in range(count):
            at = (m % per) * BASE
            pivot = packs[m // per][:, at : at + BASE]
            rows = m_ref[m, low:end, :]
            new_rows = tn_full(pivot, jnp.where(own, minus_eye, rows))
            change = tn_full(jnp.where(own, 0.0, rows), new_rows)
            m_ref[m] = jnp.where((wide >= low) & (wide < end), 0.0, m_ref[m]) - change
            m_ref[m, low:end, :] = new_rows


def slots(id_col, id_row, first, step, capacity):
    shape = (id_col.shape[0], id_row.shape[1])
    earlier = iota(shape, 0) < first + step * iota(shape, 1)
    same = (id_col == id_row) & earlier
    rank = jnp.sum(jnp.where(same, 1, 0), axis=0, keepdims=True)
    return id_row, rank


def send_x_kernel(cap, parts, me_ref, col_ref, first_ref, second_ref, x_ref, *out_refs):
    groups, per = len(out_refs), out_refs[0].shape[0]
    rows, toks = groups * per, x_ref.shape[0]
    width = x_ref.shape[1] // parts
    hot = []
    for part in range(parts):
        total = None
        for j, ids in enumerate((first_ref, second_ref)):
            expert, rank = slots(col_ref[...], ids[...], j, 2, cap)
            ahead = expert - me_ref[0]
            ahead = jnp.where(ahead < 0, ahead + groups, ahead)
            hit = iota((rows, toks), 0) == ahead * per + part * cap + rank
            hit = jnp.where(hit, 1.0, 0.0)
            total = hit if total is None else total + hit
        hot.append(total.astype(BF))
    data = jnp.concatenate([x_ref[:, p * width : (p + 1) * width] for p in range(parts)], 0)
    out = jnp.dot(jnp.concatenate(hot, 1), data, preferred_element_type=F32)
    for k, ref in enumerate(out_refs):
        ref[...] = out[k * per : (k + 1) * per].astype(BF)


def take_x_kernel(cap, parts, me_ref, *refs):
    *in_refs, out_ref = refs
    groups, (per, width) = len(in_refs), in_refs[0].shape
    data = jnp.concatenate([ref[...] for ref in in_refs], 0)
    shape = (groups * cap, groups * per)
    row = iota(shape, 0)
    source = div(row, cap)
    behind = me_ref[0] - source
    behind = jnp.where(behind < 0, behind + groups, behind)
    base = behind * per + (row - source * cap)
    for part in range(parts):
        pick = onehot(iota(shape, 1) == base + part * cap)
        got = jnp.dot(pick, data, preferred_element_type=F32)
        out_ref[:, part * width : (part + 1) * width] = got.astype(BF)


def payload_kernel(cap, rows, ng, col_ref, row_ref, g_ref, out_ref, hot_ref, add_ref):
    pair, groups = out_ref.shape[:2]
    pairs = g_ref.shape[0]
    total = groups * rows

    @pl.when(pl.program_id(0) == 0)
    def _():
        expert, rank = slots(col_ref[...], row_ref[...], 0, 1, cap)
        row = iota((total, pairs), 0)
        for part in range(ng):
            target = expert * rows + part * cap + rank
            hot_ref[:, part * pairs : (part + 1) * pairs] = onehot(row == target)
        marked = row == row_ref[...] * rows + ng * cap
        add_ref[...] = jnp.sum(jnp.where(marked, 1.0, 0.0), axis=1, keepdims=True)

    data = jnp.concatenate(
        [
            jnp.concatenate(
                [g_ref[:, (t * ng + p) * 128 : (t * ng + p + 1) * 128] for t in range(pair)], 1
            )
            for p in range(ng)
        ],
        0,
    )
    out = jnp.dot(hot_ref[...], data, preferred_element_type=F32) + add_ref[...]
    for t in range(pair):
        piece = out[:, t * 128 : (t + 1) * 128].astype(BF)
        out_ref[t] = piece.reshape(groups, rows, 128)


def set_block(m_ref, at, cov, count, level):
    eye = iota((BLK, BLK), 0) == iota((BLK, BLK), 1)
    damp = 0.05 * jnp.exp(0.4 * jnp.full((1, 1), level, F32))
    m_ref[at] = cov * (1.0 / count) + jnp.where(eye, damp, 0.0)


def hidden_kernel(cap, ng, lev_ref, in_ref, h_ref, s_ref, count_ref, m_ref):
    groups, shards, rows, _ = in_ref.shape
    live = groups * cap
    shape = (live, groups * rows)
    row = iota(shape, 0)
    source = div(row, cap)
    base = source * rows + (row - source * cap)
    pick = jnp.concatenate([onehot(iota(shape, 1) == base + p * cap) for p in range(ng)], 0)
    total = jnp.zeros((1, 128), F32)
    for s in range(shards):
        data = in_ref[:, s].reshape(groups * rows, 128)
        got = jnp.dot(pick, data, preferred_element_type=F32).astype(BF)
        for p in range(ng):
            h_ref[s * live : (s + 1) * live, p * 128 : (p + 1) * 128] = got[
                p * live : (p + 1) * live
            ]
        for g in range(groups):
            total = total + in_ref[g, s, ng * cap : ng * cap + 1, :].astype(F32)
    count_ref[...] = total
    for c in range(m_ref.shape[0]):
        part = h_ref[:, c * BLK : (c + 1) * BLK]
        cov = lax.dot_general(part, part, TN, preferred_element_type=F32)
        set_block(m_ref, c, cov, total[:, :1], lev_ref[c])
    invert_all(m_ref, m_ref.shape[0])
    s_ref[...] = -m_ref[...]


def solve_kernel(lev_ref, count_ref, x_hbm, h_ref, s_ref, out_hbm, sum_ref, x_ref, m_ref, g_ref,
                 x_sem, out_sem):
    blocks, _, width = g_ref.shape
    cuts = [slice(c * BLK, (c + 1) * BLK) for c in range(width // BLK)]

    def fetch(b):
        columns = pl.ds(b * BLK, BLK)
        return pltpu.make_async_copy(x_hbm.at[:, columns], x_ref.at[b], x_sem.at[b])

    def store(b):
        return pltpu.make_async_copy(g_ref.at[b], out_hbm.at[b], out_sem.at[b])

    for b in range(blocks):
        fetch(b).start()
    for b in range(blocks):
        fetch(b).wait()
        x = x_ref[b]
        both = lax.dot_general(
            x, jnp.concatenate([x, h_ref[...]], 1), TN, preferred_element_type=F32
        )
        set_block(m_ref, b, both[:, :BLK], count_ref[:, :1], lev_ref[b])
        g_ref[b] = both[:, BLK:]
    invert_all(m_ref, blocks)
    right = [split2(s_ref[c]) for c in range(len(cuts))]
    total = jnp.zeros((8, 128), F32)
    for b in range(blocks):
        left = split2(-m_ref[b])
        for c, cut in enumerate(cuts):
            out = dot3(left, split2(dot3(split2(g_ref[b, :, cut]), right[c])))
            g_ref[b, :, cut] = out
            square = (out * out).reshape(BLK // 8, 8, BLK).sum(axis=0)
            for k in range(BLK // 128):
                total = total + square[:, k * 128 : (k + 1) * 128]
        store(b).start()
    sum_ref[...] = total
    for b in range(blocks):
        store(b).wait()


def scale_kernel(count, norm_ref, in_ref, out_ref):
    total = jnp.sum(jnp.sum(norm_ref[...], axis=0, keepdims=True), axis=1, keepdims=True)
    out_ref[...] = (in_ref[...] * lax.rsqrt(total / count + 1e-06)).astype(BF)


def in_hbm(*arrays):
    return [pltpu.with_memory_space_constraint(array, pltpu.HBM) for array in arrays]


def full(shape):
    return pl.BlockSpec(shape, lambda *_: (0,) * len(shape))


def local(tokens_in, out_grad, expert_ids, d_levels, f_levels):
    groups, shards = lax.axis_size("expert"), lax.axis_size("shard")
    toks, width = tokens_in.shape
    ff = out_grad.shape[2]
    ff_dev = ff // shards
    cap = min(toks, max(2, 5 * toks // (2 * groups)))
    live = groups * cap
    parts = 4
    ng = ff_dev // 128
    rows = -(-(ng * cap + 1) // 16) * 16
    vm, sm = pl.BlockSpec(memory_space=pltpu.VMEM), pl.BlockSpec(memory_space=pltpu.SMEM)

    def call(kernel, mib=16, **kwargs):
        params = pltpu.CompilerParams(vmem_limit_bytes=mib << 20)
        return pl.pallas_call(kernel, compiler_params=params, **kwargs)

    id_row = expert_ids.reshape(1, 2 * toks)
    id_col = expert_ids.reshape(2 * toks, 1)
    first, second = expert_ids[:, 0].reshape(1, toks), expert_ids[:, 1].reshape(1, toks)

    me = lax.axis_index("expert").astype(jnp.int32).reshape(1)
    per = cap * parts
    x_send = call(
        functools.partial(send_x_kernel, cap, parts),
        out_shape=[jax.ShapeDtypeStruct((per, width // parts), BF)] * groups,
        in_specs=[sm] + [vm] * 4,
        name="send_x",
    )(me, id_col, first, second, tokens_in)
    x_recv = [x_send[0]] + [
        lax.ppermute(x_send[k], "expert", [(e, (e + k) % groups) for e in range(groups)])
        for k in range(1, groups)
    ]
    payload = call(
        functools.partial(payload_kernel, cap, rows, ng),
        out_shape=jax.ShapeDtypeStruct((shards, groups, rows, 128), BF),
        grid=(shards // 2,),
        in_specs=[
            full((2 * toks, 1)),
            full((1, 2 * toks)),
            pl.BlockSpec((2 * toks, 2 * ff_dev), lambda s: (0, s)),
        ],
        out_specs=pl.BlockSpec((2, groups, rows, 128), lambda s: (s, 0, 0, 0)),
        scratch_shapes=[
            pltpu.VMEM((groups * rows, ng * 2 * toks), BF),
            pltpu.VMEM((groups * rows, 1), F32),
        ],
        name="payload",
    )(id_col, id_row, out_grad.reshape(2 * toks, ff))
    received = lax.all_to_all(payload, "shard", 0, 0, tiled=True)
    received, *x_recv = lax.optimization_barrier((received, *x_recv))
    x_group = call(
        functools.partial(take_x_kernel, cap, parts),
        out_shape=jax.ShapeDtypeStruct((live, width), BF),
        in_specs=[sm] + [vm] * groups,
        name="take_x",
    )(me, *x_recv)
    rows_x = lax.all_gather(x_group, "shard", axis=0, tiled=True)

    received = lax.all_to_all(received.transpose(1, 0, 2, 3), "expert", 0, 0, tiled=True)

    hidden = ff_dev // BLK
    rows_g, inv_f, count = call(
        functools.partial(hidden_kernel, cap, ng),
        out_shape=[
            jax.ShapeDtypeStruct((shards * live, ff_dev), BF),
            jax.ShapeDtypeStruct((hidden, BLK, BLK), F32),
            jax.ShapeDtypeStruct((1, 128), F32),
        ],
        in_specs=[sm, vm],
        out_specs=(vm,) * 3,
        scratch_shapes=[pltpu.VMEM((hidden, BLK, BLK), F32)],
        name="hidden",
    )(f_levels[0].astype(F32), received)

    blocks = width // BLK
    hbm = pl.BlockSpec(memory_space=pltpu.HBM)
    precond, square = call(
        solve_kernel,
        mib=44,
        out_shape=(
            pltpu.HBM((blocks, BLK, ff_dev), F32),
            jax.ShapeDtypeStruct((8, 128), F32),
        ),
        in_specs=[sm, vm, hbm, vm, vm],
        out_specs=(hbm, vm),
        scratch_shapes=[
            pltpu.VMEM((blocks, shards * live, BLK), BF),
            pltpu.VMEM((blocks, BLK, BLK), F32),
            pltpu.VMEM((blocks, BLK, ff_dev), F32),
            pltpu.SemaphoreType.DMA((blocks,)),
            pltpu.SemaphoreType.DMA((blocks,)),
        ],
        name="solve",
    )(d_levels[0].astype(F32), count, rows_x, rows_g, inv_f)

    devices = groups * shards
    norm = jnp.sum(square, axis=0, keepdims=True)
    norm = lax.all_to_all(
        jnp.broadcast_to(norm, (devices, 128)), ("expert", "shard"), 0, 0, tiled=True
    )
    tile = width // 4
    ascent = call(
        functools.partial(scale_kernel, float(groups * width * ff)),
        out_shape=jax.ShapeDtypeStruct((width, ff_dev), BF),
        grid=(4,),
        in_specs=[full((devices, 128)), pl.BlockSpec((tile, ff_dev), lambda i: (i, 0))],
        out_specs=pl.BlockSpec((tile, ff_dev), lambda i: (i, 0)),
        name="scale",
    )(norm, *in_hbm(precond.reshape(width, ff_dev)))
    return ascent[None]


def solution(mesh):
    return jax.shard_map(
        local,
        mesh=mesh,
        in_specs=(
            P(("expert", "shard"), None),
            P(("expert", "shard"), None, None),
            P(("expert", "shard"), None),
            P("expert", None),
            P("expert", "shard"),
        ),
        out_specs=P("expert", None, "shard"),
        check_vma=False,
    )
```

```python
import functools

import jax
import jax.numpy as jnp
from jax import lax
from jax.experimental import pallas as pl
from jax.experimental.pallas import tpu as pltpu
from jax.sharding import PartitionSpec as P

BLK = 256
BASE = 32
PANEL = 8
F32 = jnp.float32
BF = jnp.bfloat16
TN = (((0,), (0,)), ((), ()))


def iota(shape, dim):
    return lax.broadcasted_iota(jnp.int32, shape, dim)


def div(value, by):
    return (value * (65536 // by + 1)) >> 16


def onehot(hit):
    return jnp.where(hit, 1.0, 0.0).astype(BF)


def split2(x):
    high = x.astype(BF)
    return high, (x - high.astype(F32)).astype(BF)


def split3(x):
    high = x.astype(BF)
    rest = x - high.astype(F32)
    mid = rest.astype(BF)
    return high, mid, (rest - mid.astype(F32)).astype(BF)


def tn_full(a, b):
    ah, am, al = split3(a)
    bh, bm, bl = split3(b)
    return lax.dot_general(
        jnp.concatenate([ah, ah, am, ah, al, am], 0),
        jnp.concatenate([bh, bm, bh, bl, bh, bm], 0),
        TN,
        preferred_element_type=F32,
    )


def dot3(a, b):
    ah, al = a
    bh, bl = b
    return jnp.dot(
        jnp.concatenate([ah, ah, al], 1),
        jnp.concatenate([bh, bl, bh], 0),
        preferred_element_type=F32,
    )


def invert_base(packs):
    lane, sub = iota((BASE, 128), 1), iota((BASE, 128), 0)
    start = (lane // BASE) * BASE
    inner = lane - start
    packs = list(packs)
    for k0 in range(0, BASE, PANEL):
        cols = [
            [jnp.take_along_axis(x, start + (k0 + j), axis=1) for j in range(PANEL)] for x in packs
        ]
        for j in range(PANEL):
            k = k0 + j
            is_col, is_row = inner == k, sub == k
            for g, x in enumerate(packs):
                col = cols[g][j]
                inv = 1.0 / col[k : k + 1, :]
                row = jnp.where(is_col[:1], 1.0, x[k : k + 1, :]) * inv
                for jj in range(j + 1, PANEL):
                    other = cols[g][jj]
                    scaled = other[k : k + 1, :] * inv
                    cols[g][jj] = jnp.where(is_row, scaled, other - col * scaled)
                packs[g] = jnp.where(is_row, row, jnp.where(is_col, 0.0, x) - col * row)
    return packs


def invert_all(m_ref, count):
    per = 128 // BASE
    lane, sub = iota((BASE, BLK), 1), iota((BASE, BLK), 0)
    wide = iota((BLK, BLK), 1)
    for low in range(0, BLK, BASE):
        end = low + BASE
        packs = [
            jnp.concatenate(
                [m_ref[min(g + j, count - 1), low:end, low:end] for j in range(per)], axis=1
            )
            for g in range(0, count, per)
        ]
        packs = invert_base(packs)
        own = (lane >= low) & (lane < end)
        minus_eye = jnp.where(lane - low == sub, -1.0, 0.0)
        for m in range(count):
            at = (m % per) * BASE
            pivot = packs[m // per][:, at : at + BASE]
            rows = m_ref[m, low:end, :]
            new_rows = tn_full(pivot, jnp.where(own, minus_eye, rows))
            change = tn_full(jnp.where(own, 0.0, rows), new_rows)
            m_ref[m] = jnp.where((wide >= low) & (wide < end), 0.0, m_ref[m]) - change
            m_ref[m, low:end, :] = new_rows


def slots(id_col, id_row, first, step, capacity):
    shape = (id_col.shape[0], id_row.shape[1])
    earlier = iota(shape, 0) < first + step * iota(shape, 1)
    same = (id_col == id_row) & earlier
    rank = jnp.sum(jnp.where(same, 1, 0), axis=0, keepdims=True)
    return id_row, rank


def send_x_kernel(cap, parts, col_ref, first_ref, second_ref, x_ref, out_ref):
    rows, toks = out_ref.shape[0], x_ref.shape[0]
    width = x_ref.shape[1] // parts
    per = cap * parts
    hot = []
    for part in range(parts):
        total = None
        for j, ids in enumerate((first_ref, second_ref)):
            expert, rank = slots(col_ref[...], ids[...], j, 2, cap)
            target = expert * per + part * cap + rank
            hit = jnp.where(iota((rows, toks), 0) == target, 1.0, 0.0)
            total = hit if total is None else total + hit
        hot.append(total.astype(BF))
    data = jnp.concatenate([x_ref[:, p * width : (p + 1) * width] for p in range(parts)], 0)
    out_ref[...] = jnp.dot(
        jnp.concatenate(hot, 1), data, preferred_element_type=F32
    ).astype(BF)


def take_x_kernel(cap, parts, in_ref, *out_refs):
    groups, per, width = in_ref.shape
    data = in_ref[...].reshape(groups * per, width)
    shape = (groups * cap, groups * per)
    row = iota(shape, 0)
    source = div(row, cap)
    base = source * per + (row - source * cap)
    for part in range(parts):
        pick = onehot(iota(shape, 1) == base + part * cap)
        rest = part * width
        got = jnp.dot(pick, data, preferred_element_type=F32).astype(BF)
        for ref in out_refs:
            if 0 <= rest < ref.shape[1]:
                ref[:, rest : rest + width] = got
            rest -= ref.shape[1]


def payload_kernel(cap, rows, ng, col_ref, row_ref, g_ref, out_ref, hot_ref, add_ref):
    pair, groups = out_ref.shape[:2]
    pairs = g_ref.shape[0]
    total = groups * rows

    @pl.when(pl.program_id(0) == 0)
    def _():
        expert, rank = slots(col_ref[...], row_ref[...], 0, 1, cap)
        row = iota((total, pairs), 0)
        for part in range(ng):
            target = expert * rows + part * cap + rank
            hot_ref[:, part * pairs : (part + 1) * pairs] = onehot(row == target)
        marked = row == row_ref[...] * rows + ng * cap
        add_ref[...] = jnp.sum(jnp.where(marked, 1.0, 0.0), axis=1, keepdims=True)

    data = jnp.concatenate(
        [
            jnp.concatenate(
                [g_ref[:, (t * ng + p) * 128 : (t * ng + p + 1) * 128] for t in range(pair)], 1
            )
            for p in range(ng)
        ],
        0,
    )
    out = jnp.dot(hot_ref[...], data, preferred_element_type=F32) + add_ref[...]
    for t in range(pair):
        piece = out[:, t * 128 : (t + 1) * 128].astype(BF)
        out_ref[t] = piece.reshape(groups, rows, 128)


def join_kernel(first_ref, second_ref, out_ref):
    rows = first_ref.shape[0]
    out_ref[:rows] = first_ref[...]
    out_ref[rows:] = second_ref[...]


def rows_kernel(cap, ng, rel_ref, in_ref, one_ref, two_ref, count_ref):
    shards, groups, rows, _ = in_ref.shape
    live = groups * cap
    shape = (live, groups * rows)
    row = iota(shape, 0)
    source = div(row, cap)
    base = source * rows + (row - source * cap)
    pick = jnp.concatenate([onehot(iota(shape, 1) == base + p * cap) for p in range(ng)], 0)
    total = jnp.zeros((1, 128), F32)
    for s in range(shards):
        data = in_ref[s].reshape(groups * rows, 128)
        got = jnp.dot(pick, data, preferred_element_type=F32).astype(BF)
        h = jnp.concatenate([got[p * live : (p + 1) * live] for p in range(ng)], 1)
        one_ref[rel_ref[s]] = h
        two_ref[rel_ref[shards + s]] = h
        for g in range(groups):
            total = total + in_ref[s, g, ng * cap : ng * cap + 1, :].astype(F32)
    count_ref[...] = total


def solve_kernel(pieces, lev_ref, count_ref, *refs):
    x_refs, refs = (refs[:pieces], refs[pieces : 2 * pieces]), refs[2 * pieces :]
    h_refs, (out_ref, sum_ref, m_ref, g_ref, sem_ref) = refs[:2], refs[2:]
    width = g_ref.shape[2]
    cuts = [slice(c * BLK, (c + 1) * BLK) for c in range(width // BLK)]
    scale = 1.0 / count_ref[:, :1]
    eye = iota((BLK, BLK), 0) == iota((BLK, BLK), 1)

    def set_block(at, cov):
        damp = 0.05 * jnp.exp(0.4 * jnp.full((1, 1), lev_ref[at], F32))
        m_ref[at] = cov * scale + jnp.where(eye, damp, 0.0)

    block = 0
    for x_pieces, h_ref in zip(x_refs, h_refs):
        h = h_ref[...].reshape(-1, width)
        for at in range(0, x_pieces[0].shape[1], BLK):
            x = jnp.concatenate([ref[:, at : at + BLK] for ref in x_pieces], 0)
            both = lax.dot_general(
                x, jnp.concatenate([x, h], 1), TN, preferred_element_type=F32
            )
            set_block(block, both[:, :BLK])
            g_ref[block] = both[:, BLK:]
            block += 1
    h = h_refs[0][...].reshape(-1, width)
    for c, cut in enumerate(cuts):
        part = h[:, cut]
        set_block(block + c, lax.dot_general(part, part, TN, preferred_element_type=F32))
    invert_all(m_ref, m_ref.shape[0])
    right = [split2(-m_ref[block + c]) for c in range(len(cuts))]
    total = jnp.zeros((8, 128), F32)

    def copy(b):
        return pltpu.make_async_copy(g_ref.at[b], out_ref.at[b], sem_ref.at[b])

    for b in range(block):
        left = split2(-m_ref[b])
        for c, cut in enumerate(cuts):
            out = dot3(left, split2(dot3(split2(g_ref[b, :, cut]), right[c])))
            g_ref[b, :, cut] = out
            square = (out * out).reshape(BLK // 8, 8, BLK).sum(axis=0)
            for k in range(BLK // 128):
                total = total + square[:, k * 128 : (k + 1) * 128]
        copy(b).start()
    sum_ref[...] = total
    for b in range(block):
        copy(b).wait()


def scale_kernel(count, norm_ref, in_ref, out_ref):
    total = jnp.sum(jnp.sum(norm_ref[...], axis=0, keepdims=True), axis=1, keepdims=True)
    out_ref[...] = (in_ref[...] * lax.rsqrt(total / count + 1e-06)).astype(BF)


SIDE = 4


def send(array, by, inner):
    pairs = []
    for at in range(SIDE * SIDE):
        out, inn = at // SIDE, at % SIDE
        if inner:
            pairs.append((at, out * SIDE + (inn + by) % SIDE))
        else:
            pairs.append((at, (out + by) % SIDE * SIDE + inn))
    return lax.ppermute(array, "shard", pairs)


def gather(arrays, other, join):
    axes = list(zip(arrays, (True, False)))
    near = lax.optimization_barrier([send(array, 1, inner) for array, inner in axes])
    *rest, other = lax.optimization_barrier(
        [send(array, k, inner) for k in (3, 2) for array, inner in axes] + [other]
    )
    halves = [
        (join(array, near[i]), join(rest[2 + i], rest[i])) for i, array in enumerate(arrays)
    ]
    pieces = []
    for (low, high), inner in zip(halves, (False, True)):
        before, after = send(low, 1, inner), send(high, 3, inner)
        far = [send(before, 1, inner), send(after, 3, inner)]
        others = send(high, 1, inner), send(low, 3, inner)
        pieces.append([low, high, before, others[0], *far, others[1], after])
    return *pieces, other


def in_hbm(*arrays):
    return [pltpu.with_memory_space_constraint(array, pltpu.HBM) for array in arrays]


def full(shape):
    return pl.BlockSpec(shape, lambda *_: (0,) * len(shape))


def local(tokens_in, out_grad, expert_ids, d_levels, f_levels):
    groups, shards = lax.axis_size("expert"), lax.axis_size("shard")
    toks, width = tokens_in.shape
    ff = out_grad.shape[2]
    ff_dev = ff // shards
    cap = min(toks, max(2, 5 * toks // (2 * groups)))
    live = groups * cap
    parts = 4
    ng = ff_dev // 128
    rows = -(-(ng * cap + 1) // 16) * 16
    vm, sm = pl.BlockSpec(memory_space=pltpu.VMEM), pl.BlockSpec(memory_space=pltpu.SMEM)

    def call(kernel, mib=16, **kwargs):
        params = pltpu.CompilerParams(vmem_limit_bytes=mib << 20)
        return pl.pallas_call(kernel, compiler_params=params, **kwargs)

    id_row = expert_ids.reshape(1, 2 * toks)
    id_col = expert_ids.reshape(2 * toks, 1)
    first, second = expert_ids[:, 0].reshape(1, toks), expert_ids[:, 1].reshape(1, toks)

    x_send = call(
        functools.partial(send_x_kernel, cap, parts),
        out_shape=jax.ShapeDtypeStruct((groups * cap * parts, width // parts), BF),
        name="send_x",
    )(id_col, first, second, tokens_in)
    x_recv = lax.all_to_all(
        x_send.reshape(groups, cap * parts, width // parts), "expert", 0, 0, tiled=True
    )
    x_one, x_two = call(
        functools.partial(take_x_kernel, cap, parts),
        out_shape=[
            jax.ShapeDtypeStruct((live, width // 2), BF),
            jax.ShapeDtypeStruct((live, width // 2), BF),
        ],
        name="take_x",
    )(x_recv)
    payload = call(
        functools.partial(payload_kernel, cap, rows, ng),
        out_shape=jax.ShapeDtypeStruct((shards, groups, rows, 128), BF),
        grid=(shards // 2,),
        in_specs=[
            full((2 * toks, 1)),
            full((1, 2 * toks)),
            pl.BlockSpec((2 * toks, 2 * ff_dev), lambda s: (0, s)),
        ],
        out_specs=pl.BlockSpec((2, groups, rows, 128), lambda s: (s, 0, 0, 0)),
        scratch_shapes=[
            pltpu.VMEM((groups * rows, ng * 2 * toks), BF),
            pltpu.VMEM((groups * rows, 1), F32),
        ],
        name="payload",
    )(id_col, id_row, out_grad.reshape(2 * toks, ff))
    join = call(
        join_kernel, out_shape=jax.ShapeDtypeStruct((2 * live, width // 2), BF), name="join"
    )
    x_one, x_two, payload = gather((x_one, x_two), payload, join)
    received = lax.all_to_all(
        payload.reshape(shards * groups, rows, 128), ("shard", "expert"), 0, 0, tiled=True
    ).reshape(shards, groups, rows, 128)

    me = lax.axis_index("shard")
    order = jnp.arange(shards, dtype=jnp.int32)
    back_out = (me // SIDE - order // SIDE) % SIDE
    back_in = (me % SIDE - order % SIDE) % SIDE
    place = jnp.concatenate([back_out * SIDE + back_in, back_in * SIDE + back_out])
    *rows_g, count = call(
        functools.partial(rows_kernel, cap, ng),
        out_shape=[jax.ShapeDtypeStruct((shards, live, ff_dev), BF)] * 2
        + [jax.ShapeDtypeStruct((1, 128), F32)],
        in_specs=[sm, vm],
        out_specs=(vm,) * 3,
        name="rows",
    )(place, received)

    blocks = width // BLK
    total = blocks + ff_dev // BLK
    precond, square = call(
        functools.partial(solve_kernel, len(x_one)),
        mib=48,
        out_shape=(
            pltpu.HBM((blocks, BLK, ff_dev), F32),
            jax.ShapeDtypeStruct((8, 128), F32),
        ),
        in_specs=[sm] + [vm] * (3 + 2 * len(x_one)),
        out_specs=(pl.BlockSpec(memory_space=pltpu.HBM), vm),
        scratch_shapes=[
            pltpu.VMEM((total, BLK, BLK), F32),
            pltpu.VMEM((blocks, BLK, ff_dev), F32),
            pltpu.SemaphoreType.DMA((blocks,)),
        ],
        name="solve",
    )(jnp.concatenate([d_levels[0], f_levels[0]]).astype(F32), count, *x_one, *x_two, *rows_g)

    devices = groups * shards
    norm = jnp.sum(square, axis=0, keepdims=True)
    norm = lax.all_to_all(
        jnp.broadcast_to(norm, (devices, 128)), ("expert", "shard"), 0, 0, tiled=True
    )
    tile = width // 4
    ascent = call(
        functools.partial(scale_kernel, float(groups * width * ff)),
        out_shape=jax.ShapeDtypeStruct((width, ff_dev), BF),
        grid=(4,),
        in_specs=[full((devices, 128)), pl.BlockSpec((tile, ff_dev), lambda i: (i, 0))],
        out_specs=pl.BlockSpec((tile, ff_dev), lambda i: (i, 0)),
        name="scale",
    )(norm, *in_hbm(precond.reshape(width, ff_dev)))
    return ascent[None]


def solution(mesh):
    return jax.shard_map(
        local,
        mesh=mesh,
        in_specs=(
            P(("expert", "shard"), None),
            P(("expert", "shard"), None, None),
            P(("expert", "shard"), None),
            P("expert", None),
            P("expert", "shard"),
        ),
        out_specs=P("expert", None, "shard"),
        check_vma=False,
    )
```

```python
import functools

import jax
import jax.numpy as jnp
from jax import lax
from jax.experimental import pallas as pl
from jax.experimental.pallas import tpu as pltpu
from jax.sharding import PartitionSpec as P

BLK = 256
BASE = 32
PANEL = 8
F32 = jnp.float32
BF = jnp.bfloat16
TN = (((0,), (0,)), ((), ()))


def iota(shape, dim):
    return lax.broadcasted_iota(jnp.int32, shape, dim)


def div(value, by):
    return (value * (65536 // by + 1)) >> 16


def onehot(hit):
    return jnp.where(hit, 1.0, 0.0).astype(BF)


def split2(x):
    high = x.astype(BF)
    return high, (x - high.astype(F32)).astype(BF)


def split3(x):
    high = x.astype(BF)
    rest = x - high.astype(F32)
    mid = rest.astype(BF)
    return high, mid, (rest - mid.astype(F32)).astype(BF)


def tn_full(a, b):
    ah, am, al = split3(a)
    bh, bm, bl = split3(b)
    return lax.dot_general(
        jnp.concatenate([ah, ah, am, ah, al, am], 0),
        jnp.concatenate([bh, bm, bh, bl, bh, bm], 0),
        TN,
        preferred_element_type=F32,
    )


def dot3(a, b):
    ah, al = a
    bh, bl = b
    return jnp.dot(
        jnp.concatenate([ah, ah, al], 1),
        jnp.concatenate([bh, bl, bh], 0),
        preferred_element_type=F32,
    )


def invert_base(packs):
    lane, sub = iota((BASE, 128), 1), iota((BASE, 128), 0)
    start = (lane // BASE) * BASE
    inner = lane - start
    packs = list(packs)
    for k0 in range(0, BASE, PANEL):
        cols = [
            [jnp.take_along_axis(x, start + (k0 + j), axis=1) for j in range(PANEL)] for x in packs
        ]
        for j in range(PANEL):
            k = k0 + j
            is_col, is_row = inner == k, sub == k
            for g, x in enumerate(packs):
                col = cols[g][j]
                inv = 1.0 / col[k : k + 1, :]
                row = jnp.where(is_col[:1], 1.0, x[k : k + 1, :]) * inv
                for jj in range(j + 1, PANEL):
                    other = cols[g][jj]
                    scaled = other[k : k + 1, :] * inv
                    cols[g][jj] = jnp.where(is_row, scaled, other - col * scaled)
                packs[g] = jnp.where(is_row, row, jnp.where(is_col, 0.0, x) - col * row)
    return packs


def invert_all(m_ref, count):
    per = 128 // BASE
    lane, sub = iota((BASE, BLK), 1), iota((BASE, BLK), 0)
    wide = iota((BLK, BLK), 1)
    for low in range(0, BLK, BASE):
        end = low + BASE
        packs = [
            jnp.concatenate(
                [m_ref[min(g + j, count - 1), low:end, low:end] for j in range(per)], axis=1
            )
            for g in range(0, count, per)
        ]
        packs = invert_base(packs)
        own = (lane >= low) & (lane < end)
        minus_eye = jnp.where(lane - low == sub, -1.0, 0.0)
        for m in range(count):
            at = (m % per) * BASE
            pivot = packs[m // per][:, at : at + BASE]
            rows = m_ref[m, low:end, :]
            new_rows = tn_full(pivot, jnp.where(own, minus_eye, rows))
            change = tn_full(jnp.where(own, 0.0, rows), new_rows)
            m_ref[m] = jnp.where((wide >= low) & (wide < end), 0.0, m_ref[m]) - change
            m_ref[m, low:end, :] = new_rows


def slots(id_col, id_row, first, step, capacity):
    shape = (id_col.shape[0], id_row.shape[1])
    earlier = iota(shape, 0) < first + step * iota(shape, 1)
    same = (id_col == id_row) & earlier
    rank = jnp.sum(jnp.where(same, 1, 0), axis=0, keepdims=True)
    return id_row, rank


def send_x_kernel(cap, parts, me_ref, col_ref, first_ref, second_ref, x_ref, *out_refs):
    groups, per = len(out_refs), out_refs[0].shape[0]
    rows, toks = groups * per, x_ref.shape[0]
    width = x_ref.shape[1] // parts
    hot = []
    for part in range(parts):
        total = None
        for j, ids in enumerate((first_ref, second_ref)):
            expert, rank = slots(col_ref[...], ids[...], j, 2, cap)
            ahead = expert - me_ref[0]
            ahead = jnp.where(ahead < 0, ahead + groups, ahead)
            hit = iota((rows, toks), 0) == ahead * per + part * cap + rank
            hit = jnp.where(hit, 1.0, 0.0)
            total = hit if total is None else total + hit
        hot.append(total.astype(BF))
    data = jnp.concatenate([x_ref[:, p * width : (p + 1) * width] for p in range(parts)], 0)
    out = jnp.dot(jnp.concatenate(hot, 1), data, preferred_element_type=F32)
    for k, ref in enumerate(out_refs):
        ref[...] = out[k * per : (k + 1) * per].astype(BF)


def take_x_kernel(cap, parts, me_ref, *refs):
    *in_refs, out_ref = refs
    groups, (per, width) = len(in_refs), in_refs[0].shape
    data = jnp.concatenate([ref[...] for ref in in_refs], 0)
    shape = (groups * cap, groups * per)
    row = iota(shape, 0)
    source = div(row, cap)
    behind = me_ref[0] - source
    behind = jnp.where(behind < 0, behind + groups, behind)
    base = behind * per + (row - source * cap)
    for part in range(parts):
        pick = onehot(iota(shape, 1) == base + part * cap)
        got = jnp.dot(pick, data, preferred_element_type=F32)
        out_ref[:, part * width : (part + 1) * width] = got.astype(BF)


def payload_kernel(cap, rows, ng, col_ref, row_ref, g_ref, out_ref, hot_ref, add_ref):
    pair, groups = out_ref.shape[:2]
    pairs = g_ref.shape[0]
    total = groups * rows

    @pl.when(pl.program_id(0) == 0)
    def _():
        expert, rank = slots(col_ref[...], row_ref[...], 0, 1, cap)
        row = iota((total, pairs), 0)
        for part in range(ng):
            target = expert * rows + part * cap + rank
            hot_ref[:, part * pairs : (part + 1) * pairs] = onehot(row == target)
        marked = row == row_ref[...] * rows + ng * cap
        add_ref[...] = jnp.sum(jnp.where(marked, 1.0, 0.0), axis=1, keepdims=True)

    data = jnp.concatenate(
        [
            jnp.concatenate(
                [g_ref[:, (t * ng + p) * 128 : (t * ng + p + 1) * 128] for t in range(pair)], 1
            )
            for p in range(ng)
        ],
        0,
    )
    out = jnp.dot(hot_ref[...], data, preferred_element_type=F32) + add_ref[...]
    for t in range(pair):
        piece = out[:, t * 128 : (t + 1) * 128].astype(BF)
        out_ref[t] = piece.reshape(groups, rows, 128)


def set_block(m_ref, at, cov, count, level):
    eye = iota((BLK, BLK), 0) == iota((BLK, BLK), 1)
    damp = 0.05 * jnp.exp(0.4 * jnp.full((1, 1), level, F32))
    m_ref[at] = cov * (1.0 / count) + jnp.where(eye, damp, 0.0)


def hidden_kernel(cap, ng, lev_ref, in_ref, h_ref, s_ref, count_ref, m_ref):
    groups, shards, rows, _ = in_ref.shape
    live = groups * cap
    shape = (live, groups * rows)
    row = iota(shape, 0)
    source = div(row, cap)
    base = source * rows + (row - source * cap)
    pick = jnp.concatenate([onehot(iota(shape, 1) == base + p * cap) for p in range(ng)], 0)
    total = jnp.zeros((1, 128), F32)
    for s in range(shards):
        data = in_ref[:, s].reshape(groups * rows, 128)
        got = jnp.dot(pick, data, preferred_element_type=F32).astype(BF)
        for p in range(ng):
            h_ref[s * live : (s + 1) * live, p * 128 : (p + 1) * 128] = got[
                p * live : (p + 1) * live
            ]
        for g in range(groups):
            total = total + in_ref[g, s, ng * cap : ng * cap + 1, :].astype(F32)
    count_ref[...] = total
    for c in range(m_ref.shape[0]):
        part = h_ref[:, c * BLK : (c + 1) * BLK]
        cov = lax.dot_general(part, part, TN, preferred_element_type=F32)
        set_block(m_ref, c, cov, total[:, :1], lev_ref[c])
    invert_all(m_ref, m_ref.shape[0])
    s_ref[...] = -m_ref[...]


def solve_kernel(lev_ref, count_ref, x_ref, h_ref, s_ref, out_hbm, sum_ref, m_ref, g_ref, out_sem):
    blocks, _, width = g_ref.shape
    cuts = [slice(c * BLK, (c + 1) * BLK) for c in range(width // BLK)]

    def store(b):
        return pltpu.make_async_copy(g_ref.at[b], out_hbm.at[b], out_sem.at[b])

    for b in range(blocks):
        x = x_ref[:, b * BLK : (b + 1) * BLK]
        both = lax.dot_general(
            x, jnp.concatenate([x, h_ref[...]], 1), TN, preferred_element_type=F32
        )
        set_block(m_ref, b, both[:, :BLK], count_ref[:, :1], lev_ref[b])
        g_ref[b] = both[:, BLK:]
    invert_all(m_ref, blocks)
    right = [split2(s_ref[c]) for c in range(len(cuts))]
    total = jnp.zeros((8, 128), F32)
    for b in range(blocks):
        left = split2(-m_ref[b])
        for c, cut in enumerate(cuts):
            out = dot3(left, split2(dot3(split2(g_ref[b, :, cut]), right[c])))
            g_ref[b, :, cut] = out
            square = (out * out).reshape(BLK // 8, 8, BLK).sum(axis=0)
            for k in range(BLK // 128):
                total = total + square[:, k * 128 : (k + 1) * 128]
        store(b).start()
    sum_ref[...] = total
    for b in range(blocks):
        store(b).wait()


def scale_kernel(count, norm_ref, in_ref, out_ref):
    total = jnp.sum(jnp.sum(norm_ref[...], axis=0, keepdims=True), axis=1, keepdims=True)
    out_ref[...] = (in_ref[...] * lax.rsqrt(total / count + 1e-06)).astype(BF)


def in_hbm(*arrays):
    return [pltpu.with_memory_space_constraint(array, pltpu.HBM) for array in arrays]


def full(shape):
    return pl.BlockSpec(shape, lambda *_: (0,) * len(shape))


def local(tokens_in, out_grad, expert_ids, d_levels, f_levels):
    groups, shards = lax.axis_size("expert"), lax.axis_size("shard")
    toks, width = tokens_in.shape
    ff = out_grad.shape[2]
    ff_dev = ff // shards
    cap = min(toks, max(2, 5 * toks // (2 * groups)))
    live = groups * cap
    parts = 4
    ng = ff_dev // 128
    rows = -(-(ng * cap + 1) // 16) * 16
    vm, sm = pl.BlockSpec(memory_space=pltpu.VMEM), pl.BlockSpec(memory_space=pltpu.SMEM)

    def call(kernel, mib=16, **kwargs):
        params = pltpu.CompilerParams(vmem_limit_bytes=mib << 20)
        return pl.pallas_call(kernel, compiler_params=params, **kwargs)

    id_row = expert_ids.reshape(1, 2 * toks)
    id_col = expert_ids.reshape(2 * toks, 1)
    first, second = expert_ids[:, 0].reshape(1, toks), expert_ids[:, 1].reshape(1, toks)

    me = lax.axis_index("expert").astype(jnp.int32).reshape(1)
    per = cap * parts
    x_send = call(
        functools.partial(send_x_kernel, cap, parts),
        out_shape=[jax.ShapeDtypeStruct((per, width // parts), BF)] * groups,
        in_specs=[sm] + [vm] * 4,
        name="send_x",
    )(me, id_col, first, second, tokens_in)
    x_recv = [x_send[0]] + [
        lax.ppermute(x_send[k], "expert", [(e, (e + k) % groups) for e in range(groups)])
        for k in range(1, groups)
    ]
    payload = call(
        functools.partial(payload_kernel, cap, rows, ng),
        out_shape=jax.ShapeDtypeStruct((shards, groups, rows, 128), BF),
        grid=(shards // 2,),
        in_specs=[
            full((2 * toks, 1)),
            full((1, 2 * toks)),
            pl.BlockSpec((2 * toks, 2 * ff_dev), lambda s: (0, s)),
        ],
        out_specs=pl.BlockSpec((2, groups, rows, 128), lambda s: (s, 0, 0, 0)),
        scratch_shapes=[
            pltpu.VMEM((groups * rows, ng * 2 * toks), BF),
            pltpu.VMEM((groups * rows, 1), F32),
        ],
        name="payload",
    )(id_col, id_row, out_grad.reshape(2 * toks, ff))
    received = lax.all_to_all(payload, "shard", 0, 0, tiled=True)
    x_group = call(
        functools.partial(take_x_kernel, cap, parts),
        out_shape=jax.ShapeDtypeStruct((live, width), BF),
        in_specs=[sm] + [vm] * groups,
        name="take_x",
    )(me, *x_recv)
    rows_x = lax.all_gather(x_group, "shard", axis=0, tiled=True)

    received = lax.all_to_all(received.transpose(1, 0, 2, 3), "expert", 0, 0, tiled=True)

    hidden = ff_dev // BLK
    rows_g, inv_f, count = call(
        functools.partial(hidden_kernel, cap, ng),
        out_shape=[
            jax.ShapeDtypeStruct((shards * live, ff_dev), BF),
            jax.ShapeDtypeStruct((hidden, BLK, BLK), F32),
            jax.ShapeDtypeStruct((1, 128), F32),
        ],
        in_specs=[sm, vm],
        out_specs=(vm,) * 3,
        scratch_shapes=[pltpu.VMEM((hidden, BLK, BLK), F32)],
        name="hidden",
    )(f_levels[0].astype(F32), received)

    blocks = width // BLK
    hbm = pl.BlockSpec(memory_space=pltpu.HBM)
    precond, square = call(
        solve_kernel,
        mib=44,
        out_shape=(
            pltpu.HBM((blocks, BLK, ff_dev), F32),
            jax.ShapeDtypeStruct((8, 128), F32),
        ),
        in_specs=[sm, vm, vm, vm, vm],
        out_specs=(hbm, vm),
        scratch_shapes=[
            pltpu.VMEM((blocks, BLK, BLK), F32),
            pltpu.VMEM((blocks, BLK, ff_dev), F32),
            pltpu.SemaphoreType.DMA((blocks,)),
        ],
        name="solve",
    )(d_levels[0].astype(F32), count, rows_x, rows_g, inv_f)

    devices = groups * shards
    norm = jnp.sum(square, axis=0, keepdims=True)
    norm = lax.all_to_all(
        jnp.broadcast_to(norm, (devices, 128)), ("expert", "shard"), 0, 0, tiled=True
    )
    tile = width // 4
    ascent = call(
        functools.partial(scale_kernel, float(groups * width * ff)),
        out_shape=jax.ShapeDtypeStruct((width, ff_dev), BF),
        grid=(4,),
        in_specs=[full((devices, 128)), pl.BlockSpec((tile, ff_dev), lambda i: (i, 0))],
        out_specs=pl.BlockSpec((tile, ff_dev), lambda i: (i, 0)),
        name="scale",
    )(norm, *in_hbm(precond.reshape(width, ff_dev)))
    return ascent[None]


def solution(mesh):
    return jax.shard_map(
        local,
        mesh=mesh,
        in_specs=(
            P(("expert", "shard"), None),
            P(("expert", "shard"), None, None),
            P(("expert", "shard"), None),
            P("expert", None),
            P("expert", "shard"),
        ),
        out_specs=P("expert", None, "shard"),
        check_vma=False,
    )
```

```python
import functools

import jax
import jax.numpy as jnp
from jax import lax
from jax.experimental import pallas as pl
from jax.experimental.pallas import tpu as pltpu
from jax.sharding import PartitionSpec as P

BLK = 256
BASE = 32
PANEL = 8
F32 = jnp.float32
BF = jnp.bfloat16
TN = (((0,), (0,)), ((), ()))


def iota(shape, dim):
    return lax.broadcasted_iota(jnp.int32, shape, dim)


def div(value, by):
    return (value * (65536 // by + 1)) >> 16


def onehot(hit):
    return jnp.where(hit, 1.0, 0.0).astype(BF)


def split2(x):
    high = x.astype(BF)
    return high, (x - high.astype(F32)).astype(BF)


def split3(x):
    high = x.astype(BF)
    rest = x - high.astype(F32)
    mid = rest.astype(BF)
    return high, mid, (rest - mid.astype(F32)).astype(BF)


def tn_full(a, b):
    ah, am, al = split3(a)
    bh, bm, bl = split3(b)
    return lax.dot_general(
        jnp.concatenate([ah, ah, am, ah, al, am], 0),
        jnp.concatenate([bh, bm, bh, bl, bh, bm], 0),
        TN,
        preferred_element_type=F32,
    )


def dot3(a, b):
    ah, al = a
    bh, bl = b
    return jnp.dot(
        jnp.concatenate([ah, ah, al], 1),
        jnp.concatenate([bh, bl, bh], 0),
        preferred_element_type=F32,
    )


def invert_base(packs):
    lane, sub = iota((BASE, 128), 1), iota((BASE, 128), 0)
    start = (lane // BASE) * BASE
    inner = lane - start
    packs = list(packs)
    for k0 in range(0, BASE, PANEL):
        cols = [
            [jnp.take_along_axis(x, start + (k0 + j), axis=1) for j in range(PANEL)] for x in packs
        ]
        for j in range(PANEL):
            k = k0 + j
            is_col, is_row = inner == k, sub == k
            for g, x in enumerate(packs):
                col = cols[g][j]
                inv = 1.0 / col[k : k + 1, :]
                row = jnp.where(is_col[:1], 1.0, x[k : k + 1, :]) * inv
                for jj in range(j + 1, PANEL):
                    other = cols[g][jj]
                    scaled = other[k : k + 1, :] * inv
                    cols[g][jj] = jnp.where(is_row, scaled, other - col * scaled)
                packs[g] = jnp.where(is_row, row, jnp.where(is_col, 0.0, x) - col * row)
    return packs


def invert_all(m_ref, count):
    per = 128 // BASE
    lane, sub = iota((BASE, BLK), 1), iota((BASE, BLK), 0)
    wide = iota((BLK, BLK), 1)
    for low in range(0, BLK, BASE):
        end = low + BASE
        packs = [
            jnp.concatenate(
                [m_ref[min(g + j, count - 1), low:end, low:end] for j in range(per)], axis=1
            )
            for g in range(0, count, per)
        ]
        packs = invert_base(packs)
        own = (lane >= low) & (lane < end)
        minus_eye = jnp.where(lane - low == sub, -1.0, 0.0)
        for m in range(count):
            at = (m % per) * BASE
            pivot = packs[m // per][:, at : at + BASE]
            rows = m_ref[m, low:end, :]
            new_rows = tn_full(pivot, jnp.where(own, minus_eye, rows))
            change = tn_full(jnp.where(own, 0.0, rows), new_rows)
            m_ref[m] = jnp.where((wide >= low) & (wide < end), 0.0, m_ref[m]) - change
            m_ref[m, low:end, :] = new_rows


def slots(id_col, id_row, first, step, capacity):
    shape = (id_col.shape[0], id_row.shape[1])
    earlier = iota(shape, 0) < first + step * iota(shape, 1)
    same = (id_col == id_row) & earlier
    rank = jnp.sum(jnp.where(same, 1, 0), axis=0, keepdims=True)
    return id_row, rank


def send_x_kernel(cap, parts, me_ref, col_ref, first_ref, second_ref, x_ref, *out_refs):
    groups, per = len(out_refs), out_refs[0].shape[0]
    rows, toks = groups * per, x_ref.shape[0]
    width = x_ref.shape[1] // parts
    hot = []
    for part in range(parts):
        total = None
        for j, ids in enumerate((first_ref, second_ref)):
            expert, rank = slots(col_ref[...], ids[...], j, 2, cap)
            ahead = expert - me_ref[0]
            ahead = jnp.where(ahead < 0, ahead + groups, ahead)
            hit = iota((rows, toks), 0) == ahead * per + part * cap + rank
            hit = jnp.where(hit, 1.0, 0.0)
            total = hit if total is None else total + hit
        hot.append(total.astype(BF))
    data = jnp.concatenate([x_ref[:, p * width : (p + 1) * width] for p in range(parts)], 0)
    out = jnp.dot(jnp.concatenate(hot, 1), data, preferred_element_type=F32)
    for k, ref in enumerate(out_refs):
        ref[...] = out[k * per : (k + 1) * per].astype(BF)


def take_x_kernel(cap, parts, me_ref, *refs):
    *in_refs, out_ref = refs
    groups, (per, width) = len(in_refs), in_refs[0].shape
    data = jnp.concatenate([ref[...] for ref in in_refs], 0)
    shape = (groups * cap, groups * per)
    row = iota(shape, 0)
    source = div(row, cap)
    behind = me_ref[0] - source
    behind = jnp.where(behind < 0, behind + groups, behind)
    base = behind * per + (row - source * cap)
    for part in range(parts):
        pick = onehot(iota(shape, 1) == base + part * cap)
        got = jnp.dot(pick, data, preferred_element_type=F32)
        out_ref[:, part * width : (part + 1) * width] = got.astype(BF)


def payload_kernel(cap, rows, ng, col_ref, row_ref, g_ref, out_ref, hot_ref, add_ref):
    pair, groups = out_ref.shape[:2]
    pairs = g_ref.shape[0]
    total = groups * rows

    @pl.when(pl.program_id(0) == 0)
    def _():
        expert, rank = slots(col_ref[...], row_ref[...], 0, 1, cap)
        row = iota((total, pairs), 0)
        for part in range(ng):
            target = expert * rows + part * cap + rank
            hot_ref[:, part * pairs : (part + 1) * pairs] = onehot(row == target)
        marked = row == row_ref[...] * rows + ng * cap
        add_ref[...] = jnp.sum(jnp.where(marked, 1.0, 0.0), axis=1, keepdims=True)

    data = jnp.concatenate(
        [
            jnp.concatenate(
                [g_ref[:, (t * ng + p) * 128 : (t * ng + p + 1) * 128] for t in range(pair)], 1
            )
            for p in range(ng)
        ],
        0,
    )
    out = jnp.dot(hot_ref[...], data, preferred_element_type=F32) + add_ref[...]
    for t in range(pair):
        piece = out[:, t * 128 : (t + 1) * 128].astype(BF)
        out_ref[t] = piece.reshape(groups, rows, 128)


def set_block(m_ref, at, cov, count, level):
    eye = iota((BLK, BLK), 0) == iota((BLK, BLK), 1)
    damp = 0.05 * jnp.exp(0.4 * jnp.full((1, 1), level, F32))
    m_ref[at] = cov * (1.0 / count) + jnp.where(eye, damp, 0.0)


def hidden_kernel(cap, ng, lev_ref, in_ref, h_ref, s_ref, count_ref, m_ref):
    groups, shards, rows, _ = in_ref.shape
    live = groups * cap
    shape = (live, groups * rows)
    row = iota(shape, 0)
    source = div(row, cap)
    base = source * rows + (row - source * cap)
    pick = jnp.concatenate([onehot(iota(shape, 1) == base + p * cap) for p in range(ng)], 0)
    total = jnp.zeros((1, 128), F32)
    for s in range(shards):
        data = in_ref[:, s].reshape(groups * rows, 128)
        got = jnp.dot(pick, data, preferred_element_type=F32).astype(BF)
        for p in range(ng):
            h_ref[s * live : (s + 1) * live, p * 128 : (p + 1) * 128] = got[
                p * live : (p + 1) * live
            ]
        for g in range(groups):
            total = total + in_ref[g, s, ng * cap : ng * cap + 1, :].astype(F32)
    count_ref[...] = total
    for c in range(m_ref.shape[0]):
        part = h_ref[:, c * BLK : (c + 1) * BLK]
        cov = lax.dot_general(part, part, TN, preferred_element_type=F32)
        set_block(m_ref, c, cov, total[:, :1], lev_ref[c])
    invert_all(m_ref, m_ref.shape[0])
    s_ref[...] = -m_ref[...]


def solve_kernel(lev_ref, count_ref, x_ref, h_ref, s_ref, out_hbm, sum_ref, both_ref, m_ref, g_ref,
                 out_sem):
    blocks, _, width = g_ref.shape
    cuts = [slice(c * BLK, (c + 1) * BLK) for c in range(width // BLK)]

    def store(b):
        return pltpu.make_async_copy(g_ref.at[b], out_hbm.at[b], out_sem.at[b])

    both_ref[:, BLK:] = h_ref[...]
    for b in range(blocks):
        x = x_ref[:, b * BLK : (b + 1) * BLK]
        both_ref[:, :BLK] = x
        both = lax.dot_general(x, both_ref[...], TN, preferred_element_type=F32)
        set_block(m_ref, b, both[:, :BLK], count_ref[:, :1], lev_ref[b])
        g_ref[b] = both[:, BLK:]
    invert_all(m_ref, blocks)
    right = [split2(s_ref[c]) for c in range(len(cuts))]
    total = jnp.zeros((8, 128), F32)
    for b in range(blocks):
        left = split2(-m_ref[b])
        for c, cut in enumerate(cuts):
            out = dot3(left, split2(dot3(split2(g_ref[b, :, cut]), right[c])))
            g_ref[b, :, cut] = out
            square = (out * out).reshape(BLK // 8, 8, BLK).sum(axis=0)
            for k in range(BLK // 128):
                total = total + square[:, k * 128 : (k + 1) * 128]
        store(b).start()
    sum_ref[...] = total
    for b in range(blocks):
        store(b).wait()


def scale_kernel(count, norm_ref, in_ref, out_ref):
    total = jnp.sum(jnp.sum(norm_ref[...], axis=0, keepdims=True), axis=1, keepdims=True)
    out_ref[...] = (in_ref[...] * lax.rsqrt(total / count + 1e-06)).astype(BF)


def in_hbm(*arrays):
    return [pltpu.with_memory_space_constraint(array, pltpu.HBM) for array in arrays]


def full(shape):
    return pl.BlockSpec(shape, lambda *_: (0,) * len(shape))


def local(tokens_in, out_grad, expert_ids, d_levels, f_levels):
    groups, shards = lax.axis_size("expert"), lax.axis_size("shard")
    toks, width = tokens_in.shape
    ff = out_grad.shape[2]
    ff_dev = ff // shards
    cap = min(toks, max(2, 5 * toks // (2 * groups)))
    live = groups * cap
    parts = 4
    ng = ff_dev // 128
    rows = -(-(ng * cap + 1) // 16) * 16
    vm, sm = pl.BlockSpec(memory_space=pltpu.VMEM), pl.BlockSpec(memory_space=pltpu.SMEM)

    def call(kernel, mib=16, **kwargs):
        params = pltpu.CompilerParams(vmem_limit_bytes=mib << 20)
        return pl.pallas_call(kernel, compiler_params=params, **kwargs)

    id_row = expert_ids.reshape(1, 2 * toks)
    id_col = expert_ids.reshape(2 * toks, 1)
    first, second = expert_ids[:, 0].reshape(1, toks), expert_ids[:, 1].reshape(1, toks)

    me = lax.axis_index("expert").astype(jnp.int32).reshape(1)
    per = cap * parts
    x_send = call(
        functools.partial(send_x_kernel, cap, parts),
        out_shape=[jax.ShapeDtypeStruct((per, width // parts), BF)] * groups,
        in_specs=[sm] + [vm] * 4,
        name="send_x",
    )(me, id_col, first, second, tokens_in)
    x_recv = [x_send[0]] + [
        lax.ppermute(x_send[k], "expert", [(e, (e + k) % groups) for e in range(groups)])
        for k in range(1, groups)
    ]
    payload = call(
        functools.partial(payload_kernel, cap, rows, ng),
        out_shape=jax.ShapeDtypeStruct((shards, groups, rows, 128), BF),
        grid=(shards // 2,),
        in_specs=[
            full((2 * toks, 1)),
            full((1, 2 * toks)),
            pl.BlockSpec((2 * toks, 2 * ff_dev), lambda s: (0, s)),
        ],
        out_specs=pl.BlockSpec((2, groups, rows, 128), lambda s: (s, 0, 0, 0)),
        scratch_shapes=[
            pltpu.VMEM((groups * rows, ng * 2 * toks), BF),
            pltpu.VMEM((groups * rows, 1), F32),
        ],
        name="payload",
    )(id_col, id_row, out_grad.reshape(2 * toks, ff))
    received = lax.all_to_all(payload, "shard", 0, 0, tiled=True)
    x_group = call(
        functools.partial(take_x_kernel, cap, parts),
        out_shape=jax.ShapeDtypeStruct((live, width), BF),
        in_specs=[sm] + [vm] * groups,
        name="take_x",
    )(me, *x_recv)
    rows_x = lax.all_gather(x_group, "shard", axis=0, tiled=True)

    received = lax.all_to_all(received.transpose(1, 0, 2, 3), "expert", 0, 0, tiled=True)

    hidden = ff_dev // BLK
    rows_g, inv_f, count = call(
        functools.partial(hidden_kernel, cap, ng),
        out_shape=[
            jax.ShapeDtypeStruct((shards * live, ff_dev), BF),
            jax.ShapeDtypeStruct((hidden, BLK, BLK), F32),
            jax.ShapeDtypeStruct((1, 128), F32),
        ],
        in_specs=[sm, vm],
        out_specs=(vm,) * 3,
        scratch_shapes=[pltpu.VMEM((hidden, BLK, BLK), F32)],
        name="hidden",
    )(f_levels[0].astype(F32), received)

    blocks = width // BLK
    hbm = pl.BlockSpec(memory_space=pltpu.HBM)
    precond, square = call(
        solve_kernel,
        mib=44,
        out_shape=(
            pltpu.HBM((blocks, BLK, ff_dev), F32),
            jax.ShapeDtypeStruct((8, 128), F32),
        ),
        in_specs=[sm, vm, vm, vm, vm],
        out_specs=(hbm, vm),
        scratch_shapes=[
            pltpu.VMEM((shards * live, BLK + ff_dev), BF),
            pltpu.VMEM((blocks, BLK, BLK), F32),
            pltpu.VMEM((blocks, BLK, ff_dev), F32),
            pltpu.SemaphoreType.DMA((blocks,)),
        ],
        name="solve",
    )(d_levels[0].astype(F32), count, rows_x, rows_g, inv_f)

    devices = groups * shards
    norm = jnp.sum(square, axis=0, keepdims=True)
    norm = lax.all_to_all(
        jnp.broadcast_to(norm, (devices, 128)), ("expert", "shard"), 0, 0, tiled=True
    )
    tile = width // 4
    ascent = call(
        functools.partial(scale_kernel, float(groups * width * ff)),
        out_shape=jax.ShapeDtypeStruct((width, ff_dev), BF),
        grid=(4,),
        in_specs=[full((devices, 128)), pl.BlockSpec((tile, ff_dev), lambda i: (i, 0))],
        out_specs=pl.BlockSpec((tile, ff_dev), lambda i: (i, 0)),
        name="scale",
    )(norm, *in_hbm(precond.reshape(width, ff_dev)))
    return ascent[None]


def solution(mesh):
    return jax.shard_map(
        local,
        mesh=mesh,
        in_specs=(
            P(("expert", "shard"), None),
            P(("expert", "shard"), None, None),
            P(("expert", "shard"), None),
            P("expert", None),
            P("expert", "shard"),
        ),
        out_specs=P("expert", None, "shard"),
        check_vma=False,
    )
```
